32 devices in a mesh: rep: 8 (over z, x), exp: 4 (over y, core).
Axes of the slice: x: 2, y: 2, z: 4, core: 2. Of those that a mesh axis runs over, the one named last changes fastest.
Arguments:
- expert_ids: int32 [8, 512, 8], P('rep', 'exp'), may hold values from 0 to 15, as said below
- route_weights: bfloat16 [8, 512, 8], P('rep', 'exp'), may hold values from 0.049804688 to 0.59765625
- out_grad: bfloat16 [8, 512, 1024], P('rep', 'exp'), may hold values from -6 to 6
- saved_inputs: bfloat16 [8, 4, 32, 1024], P('rep', 'exp'), may hold values from -6 to 6
- gate_weight: bfloat16 [4, 1024, 384], P('exp', 'rep'), may hold values from -0.1875 to 0.1875
- up_weight: bfloat16 [4, 1024, 384], P('exp', 'rep'), may hold values from -0.1875 to 0.1875
- down_weight: bfloat16 [4, 1024, 384], P('exp', 'rep'), may hold values from -0.3125 to 0.3125
Outputs:
- input_grad: bfloat16 [8, 512, 1024], P('rep', 'exp')
- route_grad: bfloat16 [8, 512, 8], P('rep', 'exp')
- gate_grad: float32 [4, 1024, 384], P('exp', 'rep')
- up_grad: float32 [4, 1024, 384], P('exp', 'rep')
- down_grad: float32 [4, 1024, 384], P('exp', 'rep')
The draws below stay inside these ranges and needn't reach their ends.
Inputs may be any that keep to these rules, and one draw needn't show every extreme that they name: `expert_ids`: each row names 8 different experts. Within each aligned block of 128 rows of one replica, an expert e with e % 4 == 0 is named at most 8 times; for every replica, some such expert is named exactly 8 times in each of its blocks.
All inputs are finite; a program needn't handle non-finite values.
Results may differ from the reference program's by a relative error of at most 0.014.
Values may be sent and summed in bfloat16 or wider, within the bound.
No kernel may reach another device: no remote copies, remote signals or barrier semaphores. Data moves between devices by JAX's collectives and lax.ppermute only.
A program may use at most 64 MiB of HBM per device.

```python
import math
import jax
import jax.numpy as jnp
from jax import lax

D_W = 1024
FF_W = 384
TOPK = 8
EXP_DEV = 4
TOK = 128
ROWS = 512
CAP = 8
SLOTS = 32
N_REP = 8
N_EXP = 4


def draw_expert_ids(key, part):
    count_key = jax.random.fold_in(key, 101)
    heavy_key = jax.random.fold_in(key, 202)
    other_key = jax.random.fold_in(key, 303)
    order_key = jax.random.fold_in(key, 404)
    counts = jax.random.randint(count_key, (N_REP, N_EXP, N_EXP), 0, CAP)
    heavy = jax.random.randint(heavy_key, (N_REP,), 0, N_EXP)
    counts = jnp.where(jnp.arange(N_EXP)[None, None, :] == heavy[:, None, None], CAP, counts)
    ends = jnp.cumsum(counts, axis=-1)
    totals = ends[..., -1]
    route_index = (jnp.arange(TOPK)[None, :] * TOK + jnp.arange(TOK)[:, None]).astype(jnp.int32)
    target = jnp.sum((ends[:, :, None, None, :] <= route_index[None, None, :, :, None]).astype(jnp.int32), axis=-1)
    live = route_index[None, None, :, :] < totals[:, :, None, None]
    window_ids = target * EXP_DEV
    other_width = (EXP_DEV - 1) * N_EXP

    def pick_others(one_key):
        return jax.random.permutation(one_key, other_width)[:TOPK]

    def pick_order(one_key):
        return jax.random.permutation(one_key, TOPK)
    other_keys = jax.random.split(other_key, N_REP * N_EXP * TOK)
    others = jax.vmap(pick_others)(other_keys).reshape(N_REP, N_EXP, TOK, TOPK)
    other_ids = others // (EXP_DEV - 1) * EXP_DEV + 1 + others % (EXP_DEV - 1)
    raw_ids = jnp.where(live, window_ids, other_ids)
    order_keys = jax.random.split(order_key, N_REP * N_EXP * TOK)
    shuffle = jax.vmap(pick_order)(order_keys).reshape(N_REP, N_EXP, TOK, TOPK)
    shuffled = jnp.take_along_axis(raw_ids, shuffle, axis=-1)
    return shuffled.reshape(N_REP, N_EXP * TOK, TOPK).astype(jnp.int32)


def spiked(drawn, own_key, source, target, shards_of, factor):
    owner, partner = [(jnp.arange(drawn.shape[dim]) // (drawn.shape[dim] // shards_of)).reshape([-1 if axis == dim else 1 for axis in range(drawn.ndim)]) for dim in (source, target)]
    chosen = jax.random.permutation(own_key, shards_of)[partner]
    strong = (owner == chosen) | (owner == (partner + shards_of // 2) % shards_of)
    return jnp.where(strong, factor * drawn, drawn)


def block_levels(own_key, extent, shards, low, top_value):
    gain, own = 1.0, jax.random.fold_in(own_key, 6)
    for dim, parts in shards:
        steps = jnp.exp(jax.random.uniform(jax.random.fold_in(own, dim), (parts,), jnp.float32, low / len(shards), top_value / len(shards)))
        gain = gain * jnp.repeat(steps, extent[dim] // parts).reshape([-1 if axis == dim else 1 for axis in range(len(extent))])
    return gain


def centred(rng, shape, scale, most, cuts=(), kind=jnp.bfloat16):
    drawn = jax.random.normal(rng, shape, jnp.float32) * scale
    if len(cuts) > 0:
        drawn = block_levels(rng, shape, cuts, -0.22, 0.18) * drawn
    return jnp.clip(drawn, min=-most, max=most).astype(kind)


def bell_draw_with(rng, shape, scale, bound, cuts, heavy, kind=jnp.bfloat16):
    array = scale * jax.random.normal(rng, shape, jnp.float32)
    if cuts:
        array = array * block_levels(rng, shape, cuts, -0.22, 0.18)
    return jnp.clip(spiked(array, jax.random.fold_in(rng, 3), *heavy), -bound, bound).astype(kind)


def setup_inputs(seed: int = 0) -> dict:
    keys = jax.random.split(jax.random.key(seed), 8)
    expert_ids = draw_expert_ids(jax.random.fold_in(keys[7], 71), 0)
    route_weights = jnp.clip(jnp.exp(math.log(0.59765625) - 2.4849066 * jax.random.uniform(keys[1], (N_REP, ROWS, TOPK), jnp.float32) ** block_levels(keys[1], (N_REP, ROWS, TOPK), ((0, 8), (1, 4)), -0.2, 0.2)), 0.049804688, 0.59765625).astype(jnp.bfloat16)
    out_grad = centred(keys[2], (N_REP, ROWS, D_W), 1.0, 6.0, ((0, 8), (1, 4)))
    saved_inputs = bell_draw_with(keys[3], (N_REP, N_EXP, SLOTS, D_W), 1.0, 6.0, ((0, 8), (1, 4)), (0, 3, 8, 2.0))
    gate_weight = centred(keys[4], (N_EXP, D_W, FF_W), D_W ** -0.5, 0.1875, ((0, 4), (1, 8)))
    up_weight = centred(keys[5], (N_EXP, D_W, FF_W), D_W ** -0.5, 0.1875, ((0, 4), (1, 8)))
    down_weight = centred(keys[6], (N_EXP, D_W, FF_W), FF_W ** -0.5, 0.3125, ((0, 4), (1, 8)))
    return dict(expert_ids=expert_ids, route_weights=route_weights, out_grad=out_grad, saved_inputs=saved_inputs, gate_weight=gate_weight, up_weight=up_weight, down_weight=down_weight)


def slot_table(block_ids):
    flat_ids = block_ids.reshape(-1)
    chosen = flat_ids % EXP_DEV == 0
    owner_of = flat_ids // EXP_DEV
    onehot = ((owner_of[:, None] == jnp.arange(N_EXP)[None, :]) & chosen[:, None]).astype(jnp.int32)
    earlier = jnp.cumsum(onehot, axis=0) - onehot
    position = jnp.sum(earlier * onehot, axis=1)
    slot_of = jnp.where(chosen, owner_of * CAP + position, -1)
    return slot_of[None, :] == jnp.arange(N_EXP * CAP)[:, None]


def expert_backward(packed):
    inputs_here, grad_rows, scale_row, gate_matrix, up_matrix, down_matrix = packed
    scale_col = scale_row[:, None].astype(jnp.float32)
    pre_gate = jnp.dot(inputs_here, gate_matrix, preferred_element_type=jnp.float32)
    pre_up = jnp.dot(inputs_here, up_matrix, preferred_element_type=jnp.float32)
    sigmoid_gate = jax.nn.sigmoid(pre_gate)
    activated = pre_gate * sigmoid_gate
    hidden = (activated * pre_up).astype(jnp.bfloat16)
    raw_grad = jnp.dot(grad_rows, down_matrix, preferred_element_type=jnp.float32)
    slot_route = jnp.sum(hidden.astype(jnp.float32) * raw_grad, axis=1).astype(jnp.bfloat16)
    hidden_grad = scale_col * raw_grad
    scaled_rows = (scale_col * grad_rows.astype(jnp.float32)).astype(jnp.bfloat16)
    gate_delta = (hidden_grad * pre_up * sigmoid_gate * (1.0 + pre_gate * (1.0 - sigmoid_gate))).astype(jnp.bfloat16)
    up_delta = (hidden_grad * activated).astype(jnp.bfloat16)
    back_rows = (jnp.dot(gate_delta, gate_matrix.T, preferred_element_type=jnp.float32)
                 + jnp.dot(up_delta, up_matrix.T, preferred_element_type=jnp.float32)).astype(jnp.bfloat16)
    gate_term = jnp.dot(inputs_here.T, gate_delta, preferred_element_type=jnp.float32)
    up_term = jnp.dot(inputs_here.T, up_delta, preferred_element_type=jnp.float32)
    down_term = jnp.dot(scaled_rows.T, hidden, preferred_element_type=jnp.float32)
    return back_rows, slot_route, gate_term, up_term, down_term


def reference(expert_ids, route_weights, out_grad, saved_inputs, gate_weight, up_weight, down_weight):
    def replica_step(totals, inputs):
        block_ids, block_weights, block_grads, block_saved = inputs
        placed = jax.vmap(slot_table)(block_ids.reshape(N_EXP, TOK, TOPK))
        weights_dev = block_weights.reshape(N_EXP, 1, TOK * TOPK)
        slot_scale = jnp.sum(jnp.where(placed, weights_dev, jnp.zeros((), block_weights.dtype)), axis=2)
        routing = jnp.any(placed.reshape(N_EXP, SLOTS, TOK, TOPK), axis=3).astype(jnp.float32)
        grads_dev = block_grads.reshape(N_EXP, TOK, D_W).astype(jnp.float32)
        routed = jnp.einsum("sqt,std->sqd", routing, grads_dev).astype(jnp.bfloat16)
        owner_rows = routed.reshape(N_EXP, N_EXP, CAP, D_W).transpose(1, 0, 2, 3).reshape(N_EXP, SLOTS, D_W)
        owner_scale = slot_scale.reshape(N_EXP, N_EXP, CAP).transpose(1, 0, 2).reshape(N_EXP, SLOTS)
        back_rows, slot_route, gate_term, up_term, down_term = lax.map(
            expert_backward, (block_saved, owner_rows, owner_scale, gate_weight, up_weight, down_weight))
        source_rows = back_rows.reshape(N_EXP, N_EXP, CAP, D_W).transpose(1, 0, 2, 3).reshape(N_EXP, SLOTS, D_W)
        source_route = slot_route.reshape(N_EXP, N_EXP, CAP).transpose(1, 0, 2).reshape(N_EXP, SLOTS)
        input_grad = jnp.einsum("sqt,sqd->std", routing, source_rows.astype(jnp.float32))
        input_grad = input_grad.astype(jnp.bfloat16).reshape(N_EXP * TOK, D_W)
        route_grad = jnp.sum(jnp.where(placed, source_route[:, :, None], jnp.zeros((), source_route.dtype)), axis=1)
        route_grad = route_grad.reshape(N_EXP * TOK, TOPK)
        totals = (totals[0] + gate_term, totals[1] + up_term, totals[2] + down_term)
        return totals, (input_grad, route_grad)

    zeros_term = jnp.zeros((N_EXP, D_W, FF_W), jnp.float32)
    totals, (input_grad, route_grad) = lax.scan(
        replica_step, (zeros_term, zeros_term, zeros_term), (expert_ids, route_weights, out_grad, saved_inputs))
    return input_grad, route_grad, totals[0] / N_REP, totals[1] / N_REP, totals[2] / N_REP
```

```python
import jax
import jax.numpy as jnp
from jax import lax
from jax.experimental import pallas as pl
from jax.experimental.pallas import tpu as pltpu
from jax.sharding import PartitionSpec as P

TOPK = 8
EXP_DEV = 4
PARTS = 4
CAP = 8
F32 = jnp.float32
BF16 = jnp.bfloat16


def dot(left, right, ldim, rdim):
    return lax.dot_general(
        left, right, (((ldim,), (rdim,)), ((), ())), preferred_element_type=F32
    )


def call(kernel, *args, out, scratch=()):
    spec = pl.BlockSpec(memory_space=pltpu.VMEM)
    return pl.pallas_call(
        kernel,
        out_shape=[jax.ShapeDtypeStruct(s, d) for s, d in out],
        in_specs=[spec] * len(args),
        out_specs=[spec] * len(out),
        scratch_shapes=list(scratch),
        compiler_params=pltpu.CompilerParams(vmem_limit_bytes=32 << 20),
    )(*args)


def position():
    rank = lax.axis_index("rep")
    return rank // PARTS, rank % PARTS


def route_kernel(ids_ref, weights_ref, grads_ref, send_ref, hits_ref):
    ids = ids_ref[...]
    weights = weights_ref[...].astype(F32)
    slots, tokens = hits_ref.shape
    capacity = CAP
    owners = slots // capacity
    hits, scales = [], []
    for j in range(owners):
        match = ids == j * EXP_DEV
        hits.append(jnp.sum(jnp.where(match, 1.0, 0.0), axis=0, keepdims=True))
        scales.append(jnp.sum(jnp.where(match, weights, 0.0), axis=0, keepdims=True))
    pad = [jnp.zeros((1, tokens), F32)] * (-owners % 8)
    hit = jnp.concatenate(hits + pad, axis=0)
    earlier = lax.broadcasted_iota(jnp.int32, (tokens, tokens), 0) < (
        lax.broadcasted_iota(jnp.int32, (tokens, tokens), 1)
    )
    place = dot(hit.astype(BF16), jnp.where(earlier, 1.0, 0.0).astype(BF16), 1, 0)
    slot = lax.broadcasted_iota(jnp.int32, (capacity, tokens), 0).astype(F32)
    chosen, scaled = [], []
    for j in range(owners):
        here = (place[j : j + 1] == slot) & (hits[j] > 0.0)
        chosen.append(jnp.where(here, 1.0, 0.0))
        scaled.append(jnp.where(here, scales[j], 0.0))
    hits_ref[...] = jnp.concatenate(chosen, axis=0).astype(BF16)
    rows = dot(
        jnp.concatenate(scaled, axis=0).astype(BF16), grads_ref[...], 1, 0
    ).astype(BF16)
    half = send_ref.shape[1]
    for q in range(2):
        for p in range(PARTS):
            start = (q * PARTS + p) * slots
            send_ref[start : start + slots, :] = rows[:, q * half : (q + 1) * half]


def weights_kernel(gate_ref, up_ref, down_ref, *rest):
    outs, flipped = rest[:PARTS], rest[PARTS]
    part = outs[0].shape[0] // 3
    _, p = position()
    for i, ref in enumerate((gate_ref, up_ref, down_ref)):
        flipped[i] = ref[...].astype(F32).T.astype(BF16)
    for k in range(PARTS):
        start = pl.multiple_of((p ^ k) * part, part)
        for i in range(3):
            outs[k][i * part : (i + 1) * part, :] = flipped[i, pl.ds(start, part), :]


def gate_up_kernel(*refs):
    weights, inputs = refs[:PARTS], refs[PARTS : 2 * PARTS]
    weight_ref, input_ref, own_ref, sent_ref = refs[2 * PARTS :]
    q, p = position()
    width = weights[0].shape[1]
    slots = inputs[0].shape[0] // 2
    for k in range(PARTS):
        other = p ^ k
        weight_ref[:, pl.ds(pl.multiple_of(other * width, width), width)] = weights[k][...]
        for h, owner in enumerate((q, 1 - q)):
            start = pl.multiple_of((owner * PARTS + other) * slots, slots)
            input_ref[pl.ds(start, slots), :] = inputs[k][h * slots : (h + 1) * slots, :]
    rows = own_ref.shape[0]
    partial = dot(weight_ref[0:rows, :], input_ref[...], 1, 1)
    own_ref[...] = partial
    sent_ref[...] = partial.astype(BF16)


def down_kernel(weight_ref, grads_ref, own_ref, sent_ref):
    rows = own_ref.shape[0]
    partial = dot(weight_ref[2 * rows : 3 * rows, :], grads_ref[...], 1, 1)
    own_ref[...] = partial
    sent_ref[...] = partial.astype(BF16)


def delta_kernel(own_ref, other_ref, down_ref, down_other_ref, weight_ref, delta_ref, back_ref):
    part = down_ref.shape[0]
    both = own_ref[...] + other_ref[...].astype(F32)
    pre_gate, pre_up = both[:part], both[part:]
    hidden_grad = down_ref[...] + down_other_ref[...].astype(F32)
    sigmoid = jax.nn.sigmoid(pre_gate)
    activated = pre_gate * sigmoid
    hidden = (activated * pre_up).astype(BF16)
    gate_delta = hidden_grad * pre_up * sigmoid * (1.0 + pre_gate * (1.0 - sigmoid))
    up_delta = hidden_grad * activated
    delta_ref[0:part, :] = gate_delta.astype(BF16)
    delta_ref[part : 2 * part, :] = up_delta.astype(BF16)
    delta_ref[2 * part :, :] = hidden
    half = weight_ref.shape[1]
    back_ref[:, :half] = dot(
        delta_ref[0 : 2 * part, :], weight_ref[0 : 2 * part, :], 0, 0
    ).astype(BF16)
    product = hidden.astype(F32) * hidden_grad
    high = product.astype(BF16)
    low = (product - high.astype(F32)).astype(BF16)
    ones = jnp.ones((part, back_ref.shape[1] - half), BF16)
    back_ref[:, half:] = (dot(high, ones, 0, 0) + dot(low, ones, 0, 0)).astype(BF16)


def grads_kernel(delta_ref, input_ref, grads_ref, *rest):
    outs, total = rest[:PARTS], rest[PARTS]
    part = delta_ref.shape[0] // 3
    width = outs[0].shape[1]
    _, p = position()
    total[0 : 2 * part, :] = dot(delta_ref[0 : 2 * part, :], input_ref[...], 1, 0).astype(BF16)
    total[2 * part :, :] = dot(delta_ref[2 * part :, :], grads_ref[...], 1, 0).astype(BF16)
    for k in range(PARTS):
        outs[k][...] = total[:, pl.ds(pl.multiple_of((p ^ k) * width, width), width)]


def tokens_kernel(ids_ref, weights_ref, hits_ref, rows_ref, input_grad_ref, route_ref):
    slots, tokens = hits_ref.shape
    group = PARTS * slots
    half = input_grad_ref.shape[1] // 2
    hits = hits_ref[...]
    tiled = jnp.concatenate([hits] * PARTS, axis=0)
    for q in range(2):
        input_grad_ref[:, q * half : (q + 1) * half] = dot(
            tiled, rows_ref[q * group : (q + 1) * group, :half], 0, 0
        ).astype(BF16)
    route = rows_ref[0:slots, half:].astype(F32)
    for p in range(1, PARTS):
        route = route + rows_ref[p * slots : (p + 1) * slots, half:].astype(F32)
    spread = hits.astype(F32) * route
    ids = ids_ref[...]
    out = jnp.zeros(ids.shape, F32)
    for j in range(slots // CAP):
        value = jnp.sum(spread[j * CAP : (j + 1) * CAP], axis=0, keepdims=True)
        out = jnp.where(ids == j * EXP_DEV, value, out)
    route_ref[...] = (out / weights_ref[...].astype(F32)).astype(BF16)


def outputs_kernel(replicas, *refs):
    parts, outs, whole = refs[:PARTS], refs[PARTS : PARTS + 3], refs[PARTS + 3]
    part = parts[0].shape[0] // 3
    _, p = position()
    for k in range(PARTS):
        start = pl.multiple_of((p ^ k) * part, part)
        for i in range(3):
            whole[i, pl.ds(start, part), :] = parts[k][i * part : (i + 1) * part, :].astype(F32)
    for i in range(3):
        outs[i][...] = whole[i].T / replicas


def body(expert_ids, route_weights, out_grad, saved_inputs, gate_weight, up_weight, down_weight):
    owners = lax.axis_size("exp")
    replicas = lax.axis_size("rep")
    tokens, features = out_grad.shape[1:]
    slots = saved_inputs.shape[2]
    width, hidden_width = gate_weight.shape[1:]
    half, part = features // 2, hidden_width // PARTS
    rows = replicas * slots

    def swap(value, mask):
        return lax.ppermute(value, "rep", [(i, i ^ mask) for i in range(replicas)])

    saved = saved_inputs[0, 0]
    q = lax.axis_index("rep") // PARTS
    mine = lax.dynamic_slice_in_dim(saved, q * half, half, axis=1)
    theirs = lax.dynamic_slice_in_dim(saved, (1 - q) * half, half, axis=1)
    theirs = swap(theirs, PARTS)
    flipped = call(
        weights_kernel,
        gate_weight[0],
        up_weight[0],
        down_weight[0],
        out=[((3 * part, width), BF16)] * PARTS,
        scratch=[pltpu.VMEM((3, hidden_width, width), BF16)],
    )
    weights = [flipped[0]] + [swap(flipped[k], k) for k in range(1, PARTS)]

    ids = expert_ids[0].T
    scales = route_weights[0].T
    sent, hits = call(
        route_kernel,
        ids,
        scales,
        out_grad[0],
        out=[((2 * PARTS * slots, half), BF16), ((slots, tokens), BF16)],
    )
    arrived = lax.all_to_all(
        sent.reshape(replicas * owners, CAP, half), ("rep", "exp"), 0, 0, tiled=True
    ).reshape(rows, half)

    pair = jnp.concatenate([mine, theirs], axis=0)
    inputs = [pair] + [swap(pair, k) for k in range(1, PARTS)]
    weight, joined, own, gate_up_sent = call(
        gate_up_kernel,
        *weights,
        *inputs,
        out=[
            ((3 * part, half), BF16),
            ((rows, half), BF16),
            ((2 * part, rows), F32),
            ((2 * part, rows), BF16),
        ],
    )
    other = swap(gate_up_sent, PARTS)
    down_own, down_sent = call(
        down_kernel, weight, arrived, out=[((part, rows), F32), ((part, rows), BF16)]
    )
    down_other = swap(down_sent, PARTS)
    delta, back = call(
        delta_kernel,
        own,
        other,
        down_own,
        down_other,
        weight,
        out=[((3 * part, rows), BF16), ((rows, half + 128), BF16)],
    )
    returned = lax.all_to_all(
        back.reshape(replicas * owners, CAP, half + 128), ("rep", "exp"), 0, 0, tiled=True
    ).reshape(rows, half + 128)
    shares = call(
        grads_kernel,
        delta,
        joined,
        arrived,
        out=[((3 * part, width), BF16)] * PARTS,
        scratch=[pltpu.VMEM((3 * part, half), BF16)],
    )
    shares = [shares[0]] + [swap(shares[k], k) for k in range(1, PARTS)]
    input_grad, route_grad = call(
        tokens_kernel,
        ids,
        scales,
        hits,
        returned,
        out=[((tokens, features), BF16), ((TOPK, tokens), BF16)],
    )
    gate_grad, up_grad, down_grad = call(
        lambda *refs: outputs_kernel(replicas, *refs),
        *shares,
        out=[((width, hidden_width), F32)] * 3,
        scratch=[pltpu.VMEM((3, hidden_width, width), F32)],
    )
    return (input_grad[None], route_grad.T[None], gate_grad[None], up_grad[None], down_grad[None])


def slot_table(block_ids, slot_count, owners):
    flat_ids = block_ids.reshape(-1)
    chosen = flat_ids % EXP_DEV == 0
    owner_of = flat_ids // EXP_DEV
    capacity = slot_count // owners
    onehot = ((owner_of[:, None] == jnp.arange(owners)[None, :]) & chosen[:, None]).astype(
        jnp.int32
    )
    earlier = jnp.cumsum(onehot, axis=0) - onehot
    position = jnp.sum(earlier * onehot, axis=1)
    slot_of = jnp.where(chosen, owner_of * capacity + position, -1)
    return slot_of[None, :] == jnp.arange(slot_count)[:, None]


def first_contract(left, right):
    return lax.dot_general(
        left, right, (((0,), (0,)), ((), ())), preferred_element_type=jnp.float32
    )


def second_contract(left, right):
    return lax.dot_general(
        left, right, (((1,), (1,)), ((), ())), preferred_element_type=jnp.float32
    )


def general_body(expert_ids, route_weights, out_grad, saved_inputs, gate_weight, up_weight, down_weight):
    owners = lax.axis_size("exp")
    replicas = lax.axis_size("rep")
    tokens_here = out_grad.shape[1]
    features = out_grad.shape[2]
    hidden_width = gate_weight.shape[2]
    slot_count = saved_inputs.shape[2]
    capacity = slot_count // owners
    placed = slot_table(expert_ids[0], slot_count, owners)
    weights_flat = route_weights[0].reshape(-1)
    slot_scale = jnp.sum(
        jnp.where(placed, weights_flat[None, :], jnp.zeros((), weights_flat.dtype)), axis=1
    )
    token_hits = jnp.any(placed.reshape(slot_count, tokens_here, TOPK), axis=2)
    token_of = jnp.sum(jnp.where(token_hits, jnp.arange(tokens_here)[None, :], 0), axis=1)
    is_live = jnp.any(token_hits, axis=1)
    routed = jnp.where(is_live[:, None], out_grad[0][token_of], jnp.zeros((), jnp.bfloat16))
    arrived, arrived_scale = (
        lax.all_to_all(
            routed.reshape(owners, capacity, features),
            "exp",
            split_axis=0,
            concat_axis=0,
            tiled=True,
        ),
        lax.all_to_all(
            slot_scale.reshape(owners, capacity), "exp", split_axis=0, concat_axis=0, tiled=True
        ),
    )
    full_gate, full_up, full_down = (
        lax.all_gather(gate_weight[0], "rep", axis=0, tiled=True),
        lax.all_gather(up_weight[0], "rep", axis=0, tiled=True),
        lax.all_gather(down_weight[0], "rep", axis=0, tiled=True),
    )
    grad_rows = arrived.reshape(slot_count, features)
    scale_col = arrived_scale.reshape(slot_count, 1).astype(jnp.float32)
    inputs_here = saved_inputs[0, 0]
    pre_gate = jnp.dot(inputs_here, full_gate, preferred_element_type=jnp.float32)
    pre_up = jnp.dot(inputs_here, full_up, preferred_element_type=jnp.float32)
    sigmoid_gate = jax.nn.sigmoid(pre_gate)
    activated = pre_gate * sigmoid_gate
    hidden = (activated * pre_up).astype(jnp.bfloat16)
    raw_grad = jnp.dot(grad_rows, full_down, preferred_element_type=jnp.float32)
    slot_route = jnp.sum(hidden.astype(jnp.float32) * raw_grad, axis=1).astype(jnp.bfloat16)
    hidden_grad = scale_col * raw_grad
    scaled_rows = (scale_col * grad_rows.astype(jnp.float32)).astype(jnp.bfloat16)
    gate_delta = (
        hidden_grad * pre_up * sigmoid_gate * (1.0 + pre_gate * (1.0 - sigmoid_gate))
    ).astype(jnp.bfloat16)
    up_delta = (hidden_grad * activated).astype(jnp.bfloat16)
    back_rows = (
        second_contract(gate_delta, full_gate) + second_contract(up_delta, full_up)
    ).astype(jnp.bfloat16)
    returned, returned_route = (
        lax.all_to_all(
            back_rows.reshape(owners, capacity, features),
            "exp",
            split_axis=0,
            concat_axis=0,
            tiled=True,
        ),
        lax.all_to_all(
            slot_route.reshape(owners, capacity), "exp", split_axis=0, concat_axis=0, tiled=True
        ),
    )
    returned_flat = returned.reshape(slot_count, features)
    route_flat = returned_route.reshape(slot_count)
    combined = jax.ops.segment_sum(
        jnp.where(is_live[:, None], returned_flat.astype(jnp.float32), 0.0),
        token_of,
        num_segments=tokens_here,
    )
    input_grad = combined.astype(jnp.bfloat16)[None]
    route_grad = jnp.sum(
        jnp.where(placed, route_flat[:, None], jnp.zeros((), jnp.bfloat16)), axis=0
    )
    route_grad = route_grad.reshape(1, tokens_here, TOPK)
    joined_share = lax.psum_scatter(
        jnp.concatenate(
            [
                jnp.concatenate(
                    [
                        first_contract(inputs_here, gate_delta),
                        first_contract(inputs_here, up_delta),
                    ],
                    axis=1,
                ),
                first_contract(scaled_rows, hidden),
            ],
            axis=1,
        ),
        "rep",
        scatter_dimension=0,
        tiled=True,
    )
    gate_share = joined_share[:, :hidden_width]
    up_share = joined_share[:, hidden_width : 2 * hidden_width]
    down_share = joined_share[:, 2 * hidden_width :]
    gate_grad = (gate_share / replicas)[None]
    up_grad = (up_share / replicas)[None]
    down_grad = (down_share / replicas)[None]
    return (input_grad, route_grad, gate_grad, up_grad, down_grad)


def solution(mesh):
    in_specs = (
        P("rep", "exp", None),
        P("rep", "exp", None),
        P("rep", "exp", None),
        P("rep", "exp", None, None),
        P("exp", "rep", None),
        P("exp", "rep", None),
        P("exp", "rep", None),
    )
    out_specs = (
        P("rep", "exp", None),
        P("rep", "exp", None),
        P("exp", "rep", None),
        P("exp", "rep", None),
        P("exp", "rep", None),
    )
    fits = mesh.shape["rep"] == 2 * PARTS
    step = body if fits else general_body
    return jax.shard_map(step, mesh=mesh, in_specs=in_specs, out_specs=out_specs, check_vma=False)
```

```python
import jax
import jax.numpy as jnp
from jax import lax
from jax.experimental import pallas as pl
from jax.experimental.pallas import tpu as pltpu
from jax.sharding import Mesh
from jax.sharding import PartitionSpec as P

TOPK = 8
EXP_DEV = 4
PARTS = 4
CAP = 8
LANES = 128
F32 = jnp.float32
BF16 = jnp.bfloat16


def dot(left, right, ldim, rdim):
    return lax.dot_general(
        left, right, (((ldim,), (rdim,)), ((), ())), preferred_element_type=F32
    )


def call(kernel, *args, out, scratch=(), space=pltpu.VMEM, after=(), cost=None):
    spec = pl.BlockSpec(memory_space=pltpu.VMEM)
    return pl.pallas_call(
        kernel,
        out_shape=[jax.ShapeDtypeStruct(s, d) for s, d in out],
        in_specs=[pl.BlockSpec(memory_space=space)] * len(args)
        + [pl.BlockSpec(memory_space=pl.ANY)] * len(after),
        out_specs=[spec] * len(out),
        scratch_shapes=list(scratch),
        cost_estimate=cost,
        compiler_params=pltpu.CompilerParams(vmem_limit_bytes=32 << 20),
    )(*args, *after)


def in_hbm(*arrays):
    return [pltpu.with_memory_space_constraint(a, pltpu.HBM) for a in arrays]


def fetch(sources, targets, sems):
    copies = [
        pltpu.make_async_copy(source, target, sems.at[n])
        for n, (source, target) in enumerate(zip(sources, targets))
    ]
    for copy in copies:
        copy.start()
    return copies


def position():
    return lax.axis_index("q"), lax.axis_index("p")


def block(index, size):
    return pl.ds(pl.multiple_of(index * size, size), size)


def spread_kernel(gate_ref, up_ref, down_ref, saved_ref, both_ref, last_ref, *rest):
    mine_ref, across_ref, saved, sems = rest
    hidden = gate_ref.shape[1]
    half = mine_ref.shape[1]
    q, _ = position()
    targets = (both_ref.at[:, :hidden], both_ref.at[:, hidden:], last_ref)
    copies = fetch((saved_ref, gate_ref, up_ref, down_ref), (saved, *targets), sems)
    copies[0].wait()
    mine_ref[...] = saved[:, block(q, half)]
    across_ref[...] = saved[:, block(1 - q, half)]
    for copy in copies[1:]:
        copy.wait()


def route_kernel(ids_hbm, scales_hbm, grads_hbm, send_ref, hits_ref, ids_ref, scales_ref, *rest):
    grads_ref, sems = rest
    copies = fetch((ids_hbm, scales_hbm, grads_hbm), (ids_ref, scales_ref, grads_ref), sems)
    slots, tokens = hits_ref.shape
    owners = slots // CAP
    half = send_ref.shape[1]
    earlier = lax.broadcasted_iota(jnp.int32, (tokens, tokens), 0) < (
        lax.broadcasted_iota(jnp.int32, (tokens, tokens), 1)
    )
    before = jnp.where(earlier, 1.0, 0.0).astype(BF16)
    slot = lax.broadcasted_iota(jnp.int32, (CAP, tokens), 0).astype(F32)
    copies[0].wait()
    copies[1].wait()
    ids = ids_ref[...]
    weights = scales_ref[...].astype(F32)
    hits, scales = [], []
    for j in range(owners):
        match = ids == j * EXP_DEV
        hits.append(jnp.sum(jnp.where(match, 1.0, 0.0), axis=0, keepdims=True))
        scales.append(jnp.sum(jnp.where(match, weights, 0.0), axis=0, keepdims=True))
    pad = [jnp.zeros((1, tokens), F32)] * (-owners % 8)
    hit = jnp.concatenate(hits + pad, axis=0)
    place = dot(hit.astype(BF16), before, 1, 0)
    chosen, scaled = [], []
    for j in range(owners):
        here = (place[j : j + 1] == slot) & (hits[j] > 0.0)
        chosen.append(jnp.where(here, 1.0, 0.0))
        scaled.append(jnp.where(here, scales[j], 0.0))
    hits_ref[...] = jnp.concatenate(chosen, axis=0).astype(BF16)
    picks = jnp.concatenate(scaled, axis=0).astype(BF16)
    copies[2].wait()
    rows = dot(picks, grads_ref[...], 1, 0).astype(BF16)
    for h in range(2):
        send_ref[h * slots : (h + 1) * slots, :] = rows[:, h * half : (h + 1) * half]


def gate_up_kernel(mine_ref, theirs_ref, *refs):
    weights, (pair_ref, own_ref, sent_ref) = refs[:PARTS], refs[PARTS:]
    q, p = position()
    slots = mine_ref.shape[0]
    width = weights[0].shape[0]
    pair_ref[block(q, slots), :] = mine_ref[...]
    pair_ref[block(1 - q, slots), :] = theirs_ref[...]
    total = None
    for k in range(PARTS):
        term = dot(pair_ref[:, block(p ^ k, width)], weights[k][...], 1, 0)
        total = term if total is None else total + term
    own_ref[...] = total
    sent_ref[...] = total.astype(BF16)


def down_kernel(routed_ref, *refs):
    weights, (own_ref, sent_ref) = refs[:PARTS], refs[PARTS:]
    _, p = position()
    width = weights[0].shape[0]
    total = None
    for k in range(PARTS):
        term = dot(routed_ref[:, block(p ^ k, width)], weights[k][...], 1, 0)
        total = term if total is None else total + term
    own_ref[...] = total
    sent_ref[...] = total.astype(BF16)


def delta_kernel(gate_up_ref, other_ref, down_ref, down_other_ref, pair_ref, routed_ref, *refs):
    weights, back_ref, sends = refs[:PARTS], refs[PARTS], refs[PARTS + 1 :]
    _, p = position()
    width = weights[0].shape[0]
    hidden_width = down_ref.shape[1]
    half = pair_ref.shape[1]
    both = gate_up_ref[...] + other_ref[...].astype(F32)
    hidden_grad = down_ref[...] + down_other_ref[...].astype(F32)
    pre_gate, pre_up = both[:, :hidden_width], both[:, hidden_width:]
    sigmoid = jax.nn.sigmoid(pre_gate)
    activated = pre_gate * sigmoid
    hidden = (activated * pre_up).astype(BF16)
    gate_delta = hidden_grad * pre_up * sigmoid * (1.0 + pre_gate * (1.0 - sigmoid))
    gate_delta = gate_delta.astype(BF16)
    up_delta = (hidden_grad * activated).astype(BF16)
    route = jnp.sum(hidden.astype(F32) * hidden_grad, axis=1, keepdims=True)
    back_ref[:, half:] = jnp.broadcast_to(route, (route.shape[0], LANES)).astype(BF16)
    for k in range(PARTS):
        lanes = block(p ^ k, width)
        back_ref[:, lanes] = (
            dot(gate_delta, weights[k][:, :hidden_width], 1, 1)
            + dot(up_delta, weights[k][:, hidden_width : 2 * hidden_width], 1, 1)
        ).astype(BF16)
        sends[k][:, :hidden_width] = gate_delta
        sends[k][:, hidden_width : 2 * hidden_width] = up_delta
        sends[k][:, 2 * hidden_width : 3 * hidden_width] = hidden
        sends[k][:, 3 * hidden_width : 3 * hidden_width + width] = pair_ref[:, lanes]
        sends[k][:, 3 * hidden_width + width :] = routed_ref[:, lanes]


def grads_step(replicas):
    def grads_kernel(*refs):
        parts, outs = refs[:PARTS], refs[PARTS:]
        hidden_width = outs[0].shape[1]
        width = outs[0].shape[0]
        start = 3 * hidden_width
        for i in range(3):
            first = start if i < 2 else start + width
            total = None
            for part in parts:
                term = dot(
                    part[:, first : first + width],
                    part[:, i * hidden_width : (i + 1) * hidden_width],
                    0,
                    0,
                )
                total = term if total is None else total + term
            outs[i][...] = total / replicas

    return grads_kernel


def tokens_kernel(ids_ref, scales_ref, hits_ref, rows_ref, _, input_grad_ref, route_ref):
    slots = hits_ref.shape[0]
    half = input_grad_ref.shape[1] // 2
    hits = hits_ref[...]
    for h in range(2):
        input_grad_ref[:, h * half : (h + 1) * half] = dot(
            hits, rows_ref[h * slots : (h + 1) * slots, :half], 0, 0
        ).astype(BF16)
    spread = hits.astype(F32) * rows_ref[0:slots, half:].astype(F32)
    ids = ids_ref[...]
    out = jnp.zeros(ids.shape, F32)
    for j in range(slots // CAP):
        value = jnp.sum(spread[j * CAP : (j + 1) * CAP], axis=0, keepdims=True)
        out = jnp.where(ids == j * EXP_DEV, value, out)
    route_ref[...] = (out / scales_ref[...].astype(F32)).astype(BF16)


def body(expert_ids, route_weights, out_grad, saved_inputs, gate_weight, up_weight, down_weight):
    owners = lax.axis_size("exp")
    replicas = lax.axis_size("q") * PARTS
    tokens, features = out_grad.shape[1:]
    slots = saved_inputs.shape[2]
    width, hidden_width = gate_weight.shape[1:]
    half, rows = features // 2, 2 * slots

    def in_half(value, mask):
        return lax.ppermute(value, "p", [(i, i ^ mask) for i in range(PARTS)])

    def across_halves(value):
        return lax.ppermute(value, "q", [(0, 1), (1, 0)])

    def exchange(value):
        blocks = value.reshape(2 * owners, CAP, value.shape[1])
        return lax.all_to_all(blocks, ("q", "exp"), 0, 0, tiled=True).reshape(value.shape)

    both, last, mine, across = call(
        spread_kernel,
        *in_hbm(gate_weight[0], up_weight[0], down_weight[0], saved_inputs[0, 0]),
        out=[((width, 2 * hidden_width), BF16), ((width, hidden_width), BF16)]
        + [((slots, half), BF16)] * 2,
        scratch=[pltpu.VMEM((slots, features), BF16), pltpu.SemaphoreType.DMA((4,))],
        space=pltpu.HBM,
    )
    theirs = across_halves(across)
    both = [both] + [in_half(both, k) for k in range(1, PARTS)]
    last = [last] + [in_half(last, k) for k in range(1, PARTS)]
    sent, hits, ids, scales = call(
        route_kernel,
        *in_hbm(expert_ids[0].T, route_weights[0].T, out_grad[0]),
        out=[
            ((rows, half), BF16),
            ((slots, tokens), BF16),
            ((TOPK, tokens), jnp.int32),
            ((TOPK, tokens), BF16),
        ],
        scratch=[pltpu.VMEM((tokens, features), BF16), pltpu.SemaphoreType.DMA((3,))],
        space=pltpu.HBM,
    )
    routed = exchange(sent)
    pair, gate_up, partial = call(
        gate_up_kernel,
        mine,
        theirs,
        *both,
        out=[
            ((rows, half), BF16),
            ((rows, 2 * hidden_width), F32),
            ((rows, 2 * hidden_width), BF16),
        ],
    )
    other = across_halves(partial)
    down, partial = call(
        down_kernel,
        routed,
        *last,
        out=[((rows, hidden_width), F32), ((rows, hidden_width), BF16)],
    )
    back, *sends = call(
        delta_kernel,
        gate_up,
        other,
        down,
        across_halves(partial),
        pair,
        routed,
        *both,
        out=[((rows, half + LANES), BF16)]
        + [((rows, 3 * hidden_width + 2 * width), BF16)] * PARTS,
    )
    returned = exchange(back)
    sends = [sends[0]] + [in_half(sends[k], k) for k in range(1, PARTS)]
    gate_grad, up_grad, down_grad = call(
        grads_step(replicas), *sends, out=[((width, hidden_width), F32)] * 3
    )
    input_grad, route_grad = call(
        tokens_kernel,
        ids,
        scales,
        hits,
        returned,
        after=in_hbm(gate_grad),
        out=[((tokens, features), BF16), ((TOPK, tokens), BF16)],
    )
    return (input_grad[None], route_grad.T[None], gate_grad[None], up_grad[None], down_grad[None])


def slot_table(block_ids, slot_count, owners):
    flat_ids = block_ids.reshape(-1)
    chosen = flat_ids % EXP_DEV == 0
    owner_of = flat_ids // EXP_DEV
    capacity = slot_count // owners
    onehot = ((owner_of[:, None] == jnp.arange(owners)[None, :]) & chosen[:, None]).astype(
        jnp.int32
    )
    earlier = jnp.cumsum(onehot, axis=0) - onehot
    position = jnp.sum(earlier * onehot, axis=1)
    slot_of = jnp.where(chosen, owner_of * capacity + position, -1)
    return slot_of[None, :] == jnp.arange(slot_count)[:, None]


def first_contract(left, right):
    return lax.dot_general(
        left, right, (((0,), (0,)), ((), ())), preferred_element_type=jnp.float32
    )


def second_contract(left, right):
    return lax.dot_general(
        left, right, (((1,), (1,)), ((), ())), preferred_element_type=jnp.float32
    )


def general_body(expert_ids, route_weights, out_grad, saved_inputs, gate_weight, up_weight, down_weight):
    owners = lax.axis_size("exp")
    replicas = lax.axis_size("rep")
    tokens_here = out_grad.shape[1]
    features = out_grad.shape[2]
    hidden_width = gate_weight.shape[2]
    slot_count = saved_inputs.shape[2]
    capacity = slot_count // owners
    placed = slot_table(expert_ids[0], slot_count, owners)
    weights_flat = route_weights[0].reshape(-1)
    slot_scale = jnp.sum(
        jnp.where(placed, weights_flat[None, :], jnp.zeros((), weights_flat.dtype)), axis=1
    )
    token_hits = jnp.any(placed.reshape(slot_count, tokens_here, TOPK), axis=2)
    token_of = jnp.sum(jnp.where(token_hits, jnp.arange(tokens_here)[None, :], 0), axis=1)
    is_live = jnp.any(token_hits, axis=1)
    routed = jnp.where(is_live[:, None], out_grad[0][token_of], jnp.zeros((), jnp.bfloat16))
    arrived, arrived_scale = (
        lax.all_to_all(
            routed.reshape(owners, capacity, features),
            "exp",
            split_axis=0,
            concat_axis=0,
            tiled=True,
        ),
        lax.all_to_all(
            slot_scale.reshape(owners, capacity), "exp", split_axis=0, concat_axis=0, tiled=True
        ),
    )
    full_gate, full_up, full_down = (
        lax.all_gather(gate_weight[0], "rep", axis=0, tiled=True),
        lax.all_gather(up_weight[0], "rep", axis=0, tiled=True),
        lax.all_gather(down_weight[0], "rep", axis=0, tiled=True),
    )
    grad_rows = arrived.reshape(slot_count, features)
    scale_col = arrived_scale.reshape(slot_count, 1).astype(jnp.float32)
    inputs_here = saved_inputs[0, 0]
    pre_gate = jnp.dot(inputs_here, full_gate, preferred_element_type=jnp.float32)
    pre_up = jnp.dot(inputs_here, full_up, preferred_element_type=jnp.float32)
    sigmoid_gate = jax.nn.sigmoid(pre_gate)
    activated = pre_gate * sigmoid_gate
    hidden = (activated * pre_up).astype(jnp.bfloat16)
    raw_grad = jnp.dot(grad_rows, full_down, preferred_element_type=jnp.float32)
    slot_route = jnp.sum(hidden.astype(jnp.float32) * raw_grad, axis=1).astype(jnp.bfloat16)
    hidden_grad = scale_col * raw_grad
    scaled_rows = (scale_col * grad_rows.astype(jnp.float32)).astype(jnp.bfloat16)
    gate_delta = (
        hidden_grad * pre_up * sigmoid_gate * (1.0 + pre_gate * (1.0 - sigmoid_gate))
    ).astype(jnp.bfloat16)
    up_delta = (hidden_grad * activated).astype(jnp.bfloat16)
    back_rows = (
        second_contract(gate_delta, full_gate) + second_contract(up_delta, full_up)
    ).astype(jnp.bfloat16)
    returned, returned_route = (
        lax.all_to_all(
            back_rows.reshape(owners, capacity, features),
            "exp",
            split_axis=0,
            concat_axis=0,
            tiled=True,
        ),
        lax.all_to_all(
            slot_route.reshape(owners, capacity), "exp", split_axis=0, concat_axis=0, tiled=True
        ),
    )
    returned_flat = returned.reshape(slot_count, features)
    route_flat = returned_route.reshape(slot_count)
    combined = jax.ops.segment_sum(
        jnp.where(is_live[:, None], returned_flat.astype(jnp.float32), 0.0),
        token_of,
        num_segments=tokens_here,
    )
    input_grad = combined.astype(jnp.bfloat16)[None]
    route_grad = jnp.sum(
        jnp.where(placed, route_flat[:, None], jnp.zeros((), jnp.bfloat16)), axis=0
    )
    route_grad = route_grad.reshape(1, tokens_here, TOPK)
    joined_share = lax.psum_scatter(
        jnp.concatenate(
            [
                jnp.concatenate(
                    [
                        first_contract(inputs_here, gate_delta),
                        first_contract(inputs_here, up_delta),
                    ],
                    axis=1,
                ),
                first_contract(scaled_rows, hidden),
            ],
            axis=1,
        ),
        "rep",
        scatter_dimension=0,
        tiled=True,
    )
    gate_share = joined_share[:, :hidden_width]
    up_share = joined_share[:, hidden_width : 2 * hidden_width]
    down_share = joined_share[:, 2 * hidden_width :]
    gate_grad = (gate_share / replicas)[None]
    up_grad = (up_share / replicas)[None]
    down_grad = (down_share / replicas)[None]
    return (input_grad, route_grad, gate_grad, up_grad, down_grad)


def solution(mesh):
    replicas, owners = mesh.shape["rep"], mesh.shape["exp"]
    if replicas == 2 * PARTS:
        step, rep = body, ("q", "p")
        mesh = Mesh(mesh.devices.reshape(2, PARTS, owners), ("q", "p", "exp"))
    else:
        step, rep = general_body, "rep"
    in_specs = (
        P(rep, "exp", None),
        P(rep, "exp", None),
        P(rep, "exp", None),
        P(rep, "exp", None, None),
        P("exp", rep, None),
        P("exp", rep, None),
        P("exp", rep, None),
    )
    out_specs = (
        P(rep, "exp", None),
        P(rep, "exp", None),
        P("exp", rep, None),
        P("exp", rep, None),
        P("exp", rep, None),
    )
    return jax.shard_map(step, mesh=mesh, in_specs=in_specs, out_specs=out_specs, check_vma=False)
```

```python
import jax
import jax.numpy as jnp
from jax import lax
from jax.experimental import pallas as pl
from jax.experimental.pallas import tpu as pltpu
from jax.sharding import Mesh
from jax.sharding import PartitionSpec as P

TOPK = 8
EXP_DEV = 4
PARTS = 4
CAP = 8
LANES = 128
F32 = jnp.float32
RETURN_COST = pl.CostEstimate(flops=3 * 10**9, transcendentals=0, bytes_accessed=9 * 10**6)
BF16 = jnp.bfloat16


def dot(left, right, ldim, rdim):
    return lax.dot_general(
        left, right, (((ldim,), (rdim,)), ((), ())), preferred_element_type=F32
    )


def call(kernel, *args, out, scratch=(), space=pltpu.VMEM, cost=None):
    spec = pl.BlockSpec(memory_space=pltpu.VMEM)
    return pl.pallas_call(
        kernel,
        out_shape=[jax.ShapeDtypeStruct(s, d) for s, d in out],
        in_specs=[pl.BlockSpec(memory_space=space)] * len(args),
        out_specs=[spec] * len(out),
        scratch_shapes=list(scratch),
        cost_estimate=cost,
        compiler_params=pltpu.CompilerParams(vmem_limit_bytes=32 << 20),
    )(*args)


def in_hbm(*arrays):
    return [pltpu.with_memory_space_constraint(a, pltpu.HBM) for a in arrays]


def fetch(sources, targets, sems):
    copies = [
        pltpu.make_async_copy(source, target, sems.at[n])
        for n, (source, target) in enumerate(zip(sources, targets))
    ]
    for copy in copies:
        copy.start()
    return copies


def position():
    return lax.axis_index("q"), lax.axis_index("p")


def block(index, size):
    return pl.ds(pl.multiple_of(index * size, size), size)


def spread_kernel(gate_ref, up_ref, down_ref, saved_ref, whole_ref, both_ref, last_ref, *rest):
    mine_ref, across_ref, saved, sems = rest
    hidden = gate_ref.shape[1]
    half = mine_ref.shape[1]
    q, _ = position()
    targets = (both_ref.at[:, :hidden], both_ref.at[:, hidden:], last_ref)
    sources = (gate_ref, up_ref, down_ref)
    again = [whole_ref.at[:, i * hidden : (i + 1) * hidden] for i in range(3)]
    copies = fetch((saved_ref, *sources, *sources), (saved, *targets, *again), sems)
    copies[0].wait()
    mine_ref[...] = saved[:, block(q, half)]
    across_ref[...] = saved[:, block(1 - q, half)]
    for copy in copies[1:]:
        copy.wait()


def route_kernel(ids_hbm, scales_hbm, grads_hbm, send_ref, hits_ref, ids_ref, scales_ref, *rest):
    grads_ref, sems = rest
    copies = fetch((ids_hbm, scales_hbm, grads_hbm), (ids_ref, scales_ref, grads_ref), sems)
    slots, tokens = hits_ref.shape
    owners = slots // CAP
    half = send_ref.shape[1]
    earlier = lax.broadcasted_iota(jnp.int32, (tokens, tokens), 0) < (
        lax.broadcasted_iota(jnp.int32, (tokens, tokens), 1)
    )
    before = jnp.where(earlier, 1.0, 0.0).astype(BF16)
    slot = lax.broadcasted_iota(jnp.int32, (CAP, tokens), 0).astype(F32)
    copies[0].wait()
    copies[1].wait()
    ids = ids_ref[...]
    weights = scales_ref[...].astype(F32)
    hits, scales = [], []
    for j in range(owners):
        match = ids == j * EXP_DEV
        hits.append(jnp.sum(jnp.where(match, 1.0, 0.0), axis=0, keepdims=True))
        scales.append(jnp.sum(jnp.where(match, weights, 0.0), axis=0, keepdims=True))
    pad = [jnp.zeros((1, tokens), F32)] * (-owners % 8)
    hit = jnp.concatenate(hits + pad, axis=0)
    place = dot(hit.astype(BF16), before, 1, 0)
    chosen, scaled = [], []
    for j in range(owners):
        here = (place[j : j + 1] == slot) & (hits[j] > 0.0)
        chosen.append(jnp.where(here, 1.0, 0.0))
        scaled.append(jnp.where(here, scales[j], 0.0))
    hits_ref[...] = jnp.concatenate(chosen, axis=0)
    picks = jnp.concatenate(scaled, axis=0).astype(BF16)
    copies[2].wait()
    rows = dot(picks, grads_ref[...], 1, 0).astype(BF16)
    for h in range(2):
        send_ref[h * slots : (h + 1) * slots, :] = rows[:, h * half : (h + 1) * half]


def gate_up_kernel(mine_ref, theirs_ref, *refs):
    weights, (pair_ref, own_ref, sent_ref) = refs[:PARTS], refs[PARTS:]
    q, p = position()
    slots = mine_ref.shape[0]
    width = weights[0].shape[0]
    pair_ref[block(q, slots), :] = mine_ref[...]
    pair_ref[block(1 - q, slots), :] = theirs_ref[...]
    total = None
    for k in range(PARTS):
        columns = weights[k][:, : own_ref.shape[1]]
        term = dot(pair_ref[:, block(p ^ k, width)], columns, 1, 0)
        total = term if total is None else total + term
    own_ref[...] = total
    sent_ref[...] = total.astype(BF16)


def down_kernel(routed_ref, *refs):
    weights, (own_ref, sent_ref) = refs[:PARTS], refs[PARTS:]
    _, p = position()
    width = weights[0].shape[0]
    total = None
    for k in range(PARTS):
        columns = weights[k][:, weights[k].shape[1] - own_ref.shape[1] :]
        term = dot(routed_ref[:, block(p ^ k, width)], columns, 1, 0)
        total = term if total is None else total + term
    own_ref[...] = total
    sent_ref[...] = total.astype(BF16)


def delta_kernel(gate_up_ref, other_ref, down_ref, down_other_ref, pair_ref, routed_ref, *refs):
    weights, kept_ref, swap_ref, sends = refs[:PARTS], refs[PARTS], refs[PARTS + 1], refs[PARTS + 2 : -1]
    back_ref = refs[-1]
    q, p = position()
    width = weights[0].shape[0]
    hidden_width = down_ref.shape[1]
    half = pair_ref.shape[1]
    both = gate_up_ref[...] + other_ref[...].astype(F32)
    hidden_grad = down_ref[...] + down_other_ref[...].astype(F32)
    pre_gate, pre_up = both[:, :hidden_width], both[:, hidden_width:]
    sigmoid = jax.nn.sigmoid(pre_gate)
    activated = pre_gate * sigmoid
    hidden = (activated * pre_up).astype(BF16)
    gate_delta = hidden_grad * pre_up * sigmoid * (1.0 + pre_gate * (1.0 - sigmoid))
    gate_delta = gate_delta.astype(BF16)
    up_delta = (hidden_grad * activated).astype(BF16)
    route = jnp.sum(hidden.astype(F32) * hidden_grad, axis=1, keepdims=True)
    back_ref[:, half:] = jnp.broadcast_to(route, (route.shape[0], LANES)).astype(BF16)
    for k in range(PARTS):
        lanes = block(p ^ k, width)
        back_ref[:, lanes] = (
            dot(gate_delta, weights[k][:, :hidden_width], 1, 1)
            + dot(up_delta, weights[k][:, hidden_width : 2 * hidden_width], 1, 1)
        ).astype(BF16)
        sends[k][:, :hidden_width] = gate_delta
        sends[k][:, hidden_width : 2 * hidden_width] = up_delta
        sends[k][:, 2 * hidden_width : 3 * hidden_width] = hidden
        sends[k][:, 3 * hidden_width : 3 * hidden_width + width] = pair_ref[:, lanes]
        sends[k][:, 3 * hidden_width + width :] = routed_ref[:, lanes]
    slots = kept_ref.shape[0]
    kept_ref[...] = back_ref[block(q, slots), :]
    swap_ref[...] = back_ref[block(1 - q, slots), :]


def return_kernel(kept_ref, swap_ref, *refs):
    outs, rows_ref = refs[:-1], refs[-1]
    q, _ = position()
    half = kept_ref.shape[1] - LANES
    rows_ref[:, block(q, half)] = kept_ref[:, :half].astype(F32)
    rows_ref[:, block(1 - q, half)] = swap_ref[:, :half].astype(F32)
    rows_ref[:, 2 * half :] = kept_ref[:, half:].astype(F32)
    for m, out in enumerate(outs):
        out[...] = rows_ref[block(lax.axis_index("exp") ^ m, CAP), :].astype(BF16)


def grads_step(replicas):
    def grads_kernel(*refs):
        parts, outs = refs[:PARTS], refs[PARTS:]
        hidden_width = outs[0].shape[1]
        width = outs[0].shape[0]
        start = 3 * hidden_width
        for i in range(3):
            first = start if i < 2 else start + width
            total = None
            for part in parts:
                term = dot(
                    part[:, first : first + width],
                    part[:, i * hidden_width : (i + 1) * hidden_width],
                    0,
                    0,
                )
                total = term if total is None else total + term
            outs[i][...] = total / replicas

    return grads_kernel


def tokens_kernel(ids_ref, scales_ref, hits_ref, *refs):
    pieces, (input_grad_ref, route_ref) = refs[:-2], refs[-2:]
    features = input_grad_ref.shape[1]
    ids = ids_ref[...]
    out = jnp.zeros(ids.shape, F32)
    hits = []
    for m, piece in enumerate(pieces):
        expert = lax.axis_index("exp") ^ m
        hits.append(hits_ref[block(expert, CAP), :])
        value = jnp.sum(hits[m] * piece[:, features:].astype(F32), axis=0, keepdims=True)
        out = jnp.where(ids == expert * EXP_DEV, value, out)
    route_ref[...] = (out / scales_ref[...].astype(F32)).astype(BF16)
    rows = jnp.concatenate([piece[:, :features].astype(F32) for piece in pieces], axis=0)
    hits = jnp.concatenate(hits, axis=0)
    input_grad_ref[...] = dot(hits.astype(BF16), rows.astype(BF16), 0, 0).astype(BF16)


def body(expert_ids, route_weights, out_grad, saved_inputs, gate_weight, up_weight, down_weight):
    owners = lax.axis_size("exp")
    replicas = lax.axis_size("q") * PARTS
    tokens, features = out_grad.shape[1:]
    slots = saved_inputs.shape[2]
    width, hidden_width = gate_weight.shape[1:]
    half, rows = features // 2, 2 * slots

    def in_half(value, mask):
        return lax.ppermute(value, "p", [(i, i ^ mask) for i in range(PARTS)])

    def across_halves(value):
        return lax.ppermute(value, "q", [(0, 1), (1, 0)])

    def exchange(value):
        blocks = value.reshape(2 * owners, CAP, value.shape[1])
        return lax.all_to_all(blocks, ("q", "exp"), 0, 0, tiled=True).reshape(value.shape)

    whole, both, last, mine, across = call(
        spread_kernel,
        *in_hbm(gate_weight[0], up_weight[0], down_weight[0], saved_inputs[0, 0]),
        out=[((width, n * hidden_width), BF16) for n in (3, 2, 1)]
        + [((slots, half), BF16)] * 2,
        scratch=[pltpu.VMEM((slots, features), BF16), pltpu.SemaphoreType.DMA((7,))],
        space=pltpu.HBM,
    )
    theirs = across_halves(across)
    whole = in_half(whole, PARTS - 1)
    both = [both] + [in_half(both, k) for k in range(1, PARTS - 1)] + [whole]
    last = [last] + [in_half(last, k) for k in range(1, PARTS - 1)] + [whole]
    sent, hits, ids, scales = call(
        route_kernel,
        *in_hbm(expert_ids[0].T, route_weights[0].T, out_grad[0]),
        out=[
            ((rows, half), BF16),
            ((slots, tokens), F32),
            ((TOPK, tokens), jnp.int32),
            ((TOPK, tokens), BF16),
        ],
        scratch=[pltpu.VMEM((tokens, features), BF16), pltpu.SemaphoreType.DMA((3,))],
        space=pltpu.HBM,
    )
    routed = exchange(sent)
    pair, gate_up, partial = call(
        gate_up_kernel,
        mine,
        theirs,
        *both,
        out=[
            ((rows, half), BF16),
            ((rows, 2 * hidden_width), F32),
            ((rows, 2 * hidden_width), BF16),
        ],
    )
    other = across_halves(partial)
    down, partial = call(
        down_kernel,
        routed,
        *last,
        out=[((rows, hidden_width), F32), ((rows, hidden_width), BF16)],
    )
    kept, swapped, *sends = call(
        delta_kernel,
        gate_up,
        other,
        down,
        across_halves(partial),
        pair,
        routed,
        *both,
        out=[((slots, half + LANES), BF16)] * 2
        + [((rows, 3 * hidden_width + 2 * width), BF16)] * PARTS,
        scratch=[pltpu.VMEM((rows, half + LANES), BF16)],
    )
    pieces = call(
        return_kernel,
        kept,
        across_halves(swapped),
        cost=RETURN_COST,
        out=[((CAP, features + LANES), BF16)] * owners,
        scratch=[pltpu.VMEM((slots, features + LANES), F32)],
    )
    pieces = [pieces[0]] + [
        lax.ppermute(pieces[m], "exp", [(i, i ^ m) for i in range(owners)])
        for m in range(1, owners)
    ]
    sends = [sends[0]] + [in_half(sends[k], k) for k in range(1, PARTS)]
    gate_grad, up_grad, down_grad = call(
        grads_step(replicas), *sends, out=[((width, hidden_width), F32)] * 3
    )
    input_grad, route_grad = call(
        tokens_kernel,
        ids,
        scales,
        hits,
        *pieces,
        out=[((tokens, features), BF16), ((TOPK, tokens), BF16)],
    )
    return (input_grad[None], route_grad.T[None], gate_grad[None], up_grad[None], down_grad[None])


def slot_table(block_ids, slot_count, owners):
    flat_ids = block_ids.reshape(-1)
    chosen = flat_ids % EXP_DEV == 0
    owner_of = flat_ids // EXP_DEV
    capacity = slot_count // owners
    onehot = ((owner_of[:, None] == jnp.arange(owners)[None, :]) & chosen[:, None]).astype(
        jnp.int32
    )
    earlier = jnp.cumsum(onehot, axis=0) - onehot
    position = jnp.sum(earlier * onehot, axis=1)
    slot_of = jnp.where(chosen, owner_of * capacity + position, -1)
    return slot_of[None, :] == jnp.arange(slot_count)[:, None]


def first_contract(left, right):
    return lax.dot_general(
        left, right, (((0,), (0,)), ((), ())), preferred_element_type=jnp.float32
    )


def second_contract(left, right):
    return lax.dot_general(
        left, right, (((1,), (1,)), ((), ())), preferred_element_type=jnp.float32
    )


def general_body(expert_ids, route_weights, out_grad, saved_inputs, gate_weight, up_weight, down_weight):
    owners = lax.axis_size("exp")
    replicas = lax.axis_size("rep")
    tokens_here = out_grad.shape[1]
    features = out_grad.shape[2]
    hidden_width = gate_weight.shape[2]
    slot_count = saved_inputs.shape[2]
    capacity = slot_count // owners
    placed = slot_table(expert_ids[0], slot_count, owners)
    weights_flat = route_weights[0].reshape(-1)
    slot_scale = jnp.sum(
        jnp.where(placed, weights_flat[None, :], jnp.zeros((), weights_flat.dtype)), axis=1
    )
    token_hits = jnp.any(placed.reshape(slot_count, tokens_here, TOPK), axis=2)
    token_of = jnp.sum(jnp.where(token_hits, jnp.arange(tokens_here)[None, :], 0), axis=1)
    is_live = jnp.any(token_hits, axis=1)
    routed = jnp.where(is_live[:, None], out_grad[0][token_of], jnp.zeros((), jnp.bfloat16))
    arrived, arrived_scale = (
        lax.all_to_all(
            routed.reshape(owners, capacity, features),
            "exp",
            split_axis=0,
            concat_axis=0,
            tiled=True,
        ),
        lax.all_to_all(
            slot_scale.reshape(owners, capacity), "exp", split_axis=0, concat_axis=0, tiled=True
        ),
    )
    full_gate, full_up, full_down = (
        lax.all_gather(gate_weight[0], "rep", axis=0, tiled=True),
        lax.all_gather(up_weight[0], "rep", axis=0, tiled=True),
        lax.all_gather(down_weight[0], "rep", axis=0, tiled=True),
    )
    grad_rows = arrived.reshape(slot_count, features)
    scale_col = arrived_scale.reshape(slot_count, 1).astype(jnp.float32)
    inputs_here = saved_inputs[0, 0]
    pre_gate = jnp.dot(inputs_here, full_gate, preferred_element_type=jnp.float32)
    pre_up = jnp.dot(inputs_here, full_up, preferred_element_type=jnp.float32)
    sigmoid_gate = jax.nn.sigmoid(pre_gate)
    activated = pre_gate * sigmoid_gate
    hidden = (activated * pre_up).astype(jnp.bfloat16)
    raw_grad = jnp.dot(grad_rows, full_down, preferred_element_type=jnp.float32)
    slot_route = jnp.sum(hidden.astype(jnp.float32) * raw_grad, axis=1).astype(jnp.bfloat16)
    hidden_grad = scale_col * raw_grad
    scaled_rows = (scale_col * grad_rows.astype(jnp.float32)).astype(jnp.bfloat16)
    gate_delta = (
        hidden_grad * pre_up * sigmoid_gate * (1.0 + pre_gate * (1.0 - sigmoid_gate))
    ).astype(jnp.bfloat16)
    up_delta = (hidden_grad * activated).astype(jnp.bfloat16)
    back_rows = (
        second_contract(gate_delta, full_gate) + second_contract(up_delta, full_up)
    ).astype(jnp.bfloat16)
    returned, returned_route = (
        lax.all_to_all(
            back_rows.reshape(owners, capacity, features),
            "exp",
            split_axis=0,
            concat_axis=0,
            tiled=True,
        ),
        lax.all_to_all(
            slot_route.reshape(owners, capacity), "exp", split_axis=0, concat_axis=0, tiled=True
        ),
    )
    returned_flat = returned.reshape(slot_count, features)
    route_flat = returned_route.reshape(slot_count)
    combined = jax.ops.segment_sum(
        jnp.where(is_live[:, None], returned_flat.astype(jnp.float32), 0.0),
        token_of,
        num_segments=tokens_here,
    )
    input_grad = combined.astype(jnp.bfloat16)[None]
    route_grad = jnp.sum(
        jnp.where(placed, route_flat[:, None], jnp.zeros((), jnp.bfloat16)), axis=0
    )
    route_grad = route_grad.reshape(1, tokens_here, TOPK)
    joined_share = lax.psum_scatter(
        jnp.concatenate(
            [
                jnp.concatenate(
                    [
                        first_contract(inputs_here, gate_delta),
                        first_contract(inputs_here, up_delta),
                    ],
                    axis=1,
                ),
                first_contract(scaled_rows, hidden),
            ],
            axis=1,
        ),
        "rep",
        scatter_dimension=0,
        tiled=True,
    )
    gate_share = joined_share[:, :hidden_width]
    up_share = joined_share[:, hidden_width : 2 * hidden_width]
    down_share = joined_share[:, 2 * hidden_width :]
    gate_grad = (gate_share / replicas)[None]
    up_grad = (up_share / replicas)[None]
    down_grad = (down_share / replicas)[None]
    return (input_grad, route_grad, gate_grad, up_grad, down_grad)


def solution(mesh):
    replicas, owners = mesh.shape["rep"], mesh.shape["exp"]
    if replicas == 2 * PARTS:
        step, rep = body, ("q", "p")
        mesh = Mesh(mesh.devices.reshape(2, PARTS, owners), ("q", "p", "exp"))
    else:
        step, rep = general_body, "rep"
    in_specs = (
        P(rep, "exp", None),
        P(rep, "exp", None),
        P(rep, "exp", None),
        P(rep, "exp", None, None),
        P("exp", rep, None),
        P("exp", rep, None),
        P("exp", rep, None),
    )
    out_specs = (
        P(rep, "exp", None),
        P(rep, "exp", None),
        P("exp", rep, None),
        P("exp", rep, None),
        P("exp", rep, None),
    )
    return jax.shard_map(step, mesh=mesh, in_specs=in_specs, out_specs=out_specs, check_vma=False)
```

```python
import jax
import jax.numpy as jnp
from jax import lax
from jax.experimental import pallas as pl
from jax.experimental.pallas import tpu as pltpu
from jax.sharding import Mesh
from jax.sharding import PartitionSpec as P

TOPK = 8
EXP_DEV = 4
PARTS = 4
CUT = 3
CAP = 8
LANES = 128
F32 = jnp.float32
BF16 = jnp.bfloat16


def dot(left, right, ldim, rdim):
    return lax.dot_general(
        left, right, (((ldim,), (rdim,)), ((), ())), preferred_element_type=F32
    )


def call(kernel, *args, out, scratch=(), space=pltpu.VMEM, busy_us=None):
    spec = pl.BlockSpec(memory_space=pltpu.VMEM)
    return pl.pallas_call(
        kernel,
        out_shape=[jax.ShapeDtypeStruct(s, d) for s, d in out],
        in_specs=[pl.BlockSpec(memory_space=space)] * len(args),
        out_specs=[spec] * len(out),
        scratch_shapes=list(scratch),
        cost_estimate=busy_us and pl.CostEstimate(
            flops=busy_us * 10**9, transcendentals=0, bytes_accessed=busy_us * 3 * 10**6
        ),
        compiler_params=pltpu.CompilerParams(vmem_limit_bytes=32 << 20),
    )(*args)


def in_hbm(*arrays):
    return [pltpu.with_memory_space_constraint(a, pltpu.HBM) for a in arrays]


def fetch(sources, targets, sems):
    copies = [
        pltpu.make_async_copy(source, target, sems.at[n])
        for n, (source, target) in enumerate(zip(sources, targets))
    ]
    for copy in copies:
        copy.start()
    return copies


def position():
    return lax.axis_index("q"), lax.axis_index("p")


def block(index, size):
    return pl.ds(pl.multiple_of(index * size, size), size)


def spread_kernel(*refs):
    (gate_ref, up_ref, down_ref, saved_ref, ids_ref, scales_ref, grads_ref), refs = refs[:7], refs[7:]
    whole_ref, both_ref, last_ref, mine_ref, across_ref, *kept, saved, sems = refs
    hidden = gate_ref.shape[1]
    half = mine_ref.shape[1]
    q, _ = position()
    sources = (gate_ref, up_ref, down_ref)
    targets = (both_ref.at[:, :hidden], both_ref.at[:, hidden:], last_ref)
    again = [whole_ref.at[:, i * hidden : (i + 1) * hidden] for i in range(3)]
    copies = fetch(
        (saved_ref, *sources, *sources, ids_ref, scales_ref, grads_ref),
        (saved, *targets, *again, *kept),
        sems,
    )
    copies[0].wait()
    mine_ref[...] = saved[:, block(q, half)]
    across_ref[...] = saved[:, block(1 - q, half)]
    for copy in copies[1:]:
        copy.wait()


def route_kernel(ids_ref, scales_ref, grads_ref, send_ref, hits_ref):
    slots, tokens = hits_ref.shape
    owners = slots // CAP
    half = send_ref.shape[1]
    earlier = lax.broadcasted_iota(jnp.int32, (tokens, tokens), 0) < (
        lax.broadcasted_iota(jnp.int32, (tokens, tokens), 1)
    )
    before = jnp.where(earlier, 1.0, 0.0).astype(BF16)
    slot = lax.broadcasted_iota(jnp.int32, (CAP, tokens), 0).astype(F32)
    ids = ids_ref[...]
    weights = scales_ref[...].astype(F32)
    hits, scales = [], []
    for j in range(owners):
        match = ids == j * EXP_DEV
        hits.append(jnp.sum(jnp.where(match, 1.0, 0.0), axis=0, keepdims=True))
        scales.append(jnp.sum(jnp.where(match, weights, 0.0), axis=0, keepdims=True))
    pad = [jnp.zeros((1, tokens), F32)] * (-owners % 8)
    hit = jnp.concatenate(hits + pad, axis=0)
    place = dot(hit.astype(BF16), before, 1, 0)
    chosen, scaled = [], []
    for j in range(owners):
        here = (place[j : j + 1] == slot) & (hits[j] > 0.0)
        chosen.append(jnp.where(here, 1.0, 0.0))
        scaled.append(jnp.where(here, scales[j], 0.0))
    hits_ref[...] = jnp.concatenate(chosen, axis=0)
    picks = jnp.concatenate(scaled, axis=0).astype(BF16)
    rows = dot(picks, grads_ref[...], 1, 0).astype(BF16)
    for h in range(2):
        send_ref[h * slots : (h + 1) * slots, :] = rows[:, h * half : (h + 1) * half]


def gate_up_kernel(mine_ref, theirs_ref, *refs):
    weights, (pair_ref, own_ref, sent_ref) = refs[:PARTS], refs[PARTS:]
    q, p = position()
    slots = mine_ref.shape[0]
    width = weights[0].shape[0]
    pair_ref[block(q, slots), :] = mine_ref[...]
    pair_ref[block(1 - q, slots), :] = theirs_ref[...]
    total = None
    for k in range(PARTS):
        columns = weights[k][:, : own_ref.shape[1]]
        term = dot(pair_ref[:, block(p ^ k, width)], columns, 1, 0)
        total = term if total is None else total + term
    own_ref[...] = total
    sent_ref[...] = total.astype(BF16)


def down_kernel(routed_ref, *refs):
    weights, (own_ref, sent_ref) = refs[:PARTS], refs[PARTS:]
    _, p = position()
    width = weights[0].shape[0]
    total = None
    for k in range(PARTS):
        columns = weights[k][:, weights[k].shape[1] - own_ref.shape[1] :]
        term = dot(routed_ref[:, block(p ^ k, width)], columns, 1, 0)
        total = term if total is None else total + term
    own_ref[...] = total
    sent_ref[...] = total.astype(BF16)


def delta_kernel(gate_up_ref, other_ref, down_ref, down_other_ref, pair_ref, routed_ref, *refs):
    weights, kept_ref, swap_ref, sends = refs[:PARTS], refs[PARTS], refs[PARTS + 1], refs[PARTS + 2 : -1]
    back_ref = refs[-1]
    q, p = position()
    width = weights[0].shape[0]
    hidden_width = down_ref.shape[1]
    half = pair_ref.shape[1]
    both = gate_up_ref[...] + other_ref[...].astype(F32)
    hidden_grad = down_ref[...] + down_other_ref[...].astype(F32)
    pre_gate, pre_up = both[:, :hidden_width], both[:, hidden_width:]
    sigmoid = jax.nn.sigmoid(pre_gate)
    activated = pre_gate * sigmoid
    hidden = (activated * pre_up).astype(BF16)
    gate_delta = hidden_grad * pre_up * sigmoid * (1.0 + pre_gate * (1.0 - sigmoid))
    gate_delta = gate_delta.astype(BF16)
    up_delta = (hidden_grad * activated).astype(BF16)
    route = jnp.sum(hidden.astype(F32) * hidden_grad, axis=1, keepdims=True)
    back_ref[:, half:] = jnp.broadcast_to(route, (route.shape[0], LANES)).astype(BF16)
    for k in range(PARTS):
        lanes = block(p ^ k, width)
        back_ref[:, lanes] = (
            dot(gate_delta, weights[k][:, :hidden_width], 1, 1)
            + dot(up_delta, weights[k][:, hidden_width : 2 * hidden_width], 1, 1)
        ).astype(BF16)
        sends[k][:, :hidden_width] = gate_delta
        sends[k][:, hidden_width : 2 * hidden_width] = up_delta
        sends[k][:, 2 * hidden_width : 3 * hidden_width] = hidden
        sends[k][:, 3 * hidden_width : 3 * hidden_width + width] = pair_ref[:, lanes]
        sends[k][:, 3 * hidden_width + width :] = routed_ref[:, lanes]
    slots = kept_ref.shape[0]
    kept_ref[...] = back_ref[block(q, slots), :]
    swap_ref[...] = back_ref[block(1 - q, slots), :]


def return_kernel(kept_ref, swap_ref, *refs):
    outs, rows_ref = refs[:-1], refs[-1]
    q, _ = position()
    half = kept_ref.shape[1] - LANES
    rows_ref[:, block(q, half)] = kept_ref[:, :half].astype(F32)
    rows_ref[:, block(1 - q, half)] = swap_ref[:, :half].astype(F32)
    rows_ref[:, 2 * half :] = kept_ref[:, half:].astype(F32)
    for m, out in enumerate(outs):
        out[...] = rows_ref[block(lax.axis_index("exp") ^ m, CAP), :].astype(BF16)


def grads_step(replicas):
    def grads_kernel(*refs):
        parts, (gate_ref, up_ref, down_ref) = refs[:PARTS], refs[PARTS:]
        width, hidden = gate_ref.shape

        def column(start, size):
            return jnp.concatenate([part[:, start : start + size] for part in parts], axis=0)

        both = dot(column(3 * hidden, width), column(0, 2 * hidden), 0, 0) / replicas
        gate_ref[...] = both[:, :hidden]
        up_ref[...] = both[:, hidden:]
        down = dot(column(3 * hidden + width, width), column(2 * hidden, hidden), 0, 0)
        down_ref[...] = down / replicas

    return grads_kernel


def tokens_kernel(ids_ref, scales_ref, hits_ref, *refs):
    pieces, (input_grad_ref, route_ref) = refs[:-2], refs[-2:]
    features = input_grad_ref.shape[1]
    ids = ids_ref[...]
    out = jnp.zeros(ids.shape, F32)
    hits = []
    for m, piece in enumerate(pieces):
        expert = lax.axis_index("exp") ^ m
        hits.append(hits_ref[block(expert, CAP), :])
        value = jnp.sum(hits[m] * piece[:, features:].astype(F32), axis=0, keepdims=True)
        out = jnp.where(ids == expert * EXP_DEV, value, out)
    route_ref[...] = (out / scales_ref[...].astype(F32)).astype(BF16)
    rows = jnp.concatenate([piece[:, :features].astype(F32) for piece in pieces], axis=0)
    hits = jnp.concatenate(hits, axis=0)
    input_grad_ref[...] = dot(hits.astype(BF16), rows.astype(BF16), 0, 0).astype(BF16)


def body(expert_ids, route_weights, out_grad, saved_inputs, gate_weight, up_weight, down_weight):
    owners = lax.axis_size("exp")
    replicas = lax.axis_size("q") * PARTS
    tokens, features = out_grad.shape[1:]
    slots = saved_inputs.shape[2]
    width, hidden_width = gate_weight.shape[1:]
    half, rows = features // 2, 2 * slots

    def in_half(value, mask):
        return lax.ppermute(value, "p", [(i, i ^ mask) for i in range(PARTS)])

    def across_halves(value):
        return lax.ppermute(value, "q", [(0, 1), (1, 0)])

    def exchange(value):
        blocks = value.reshape(2 * owners, CAP, value.shape[1])
        return lax.all_to_all(blocks, ("q", "exp"), 0, 0, tiled=True).reshape(value.shape)

    whole, both, last, mine, across, ids, scales, grads = call(
        spread_kernel,
        *in_hbm(gate_weight[0], up_weight[0], down_weight[0], saved_inputs[0, 0]),
        *in_hbm(expert_ids[0].T, route_weights[0].T, out_grad[0]),
        out=[((width, n * hidden_width), BF16) for n in (3, 2, 1)]
        + [((slots, half), BF16)] * 2
        + [((TOPK, tokens), jnp.int32), ((TOPK, tokens), BF16), ((tokens, features), BF16)],
        scratch=[pltpu.VMEM((slots, features), BF16), pltpu.SemaphoreType.DMA((10,))],
        space=pltpu.HBM,
    )
    theirs = across_halves(across)
    wholes = {k: in_half(whole, k) for k in range(1, PARTS) if k != CUT}
    both = [both] + [wholes[k] if k in wholes else in_half(both, k) for k in range(1, PARTS)]
    last = [last] + [wholes[k] if k in wholes else in_half(last, k) for k in range(1, PARTS)]
    sent, hits = call(
        route_kernel,
        ids,
        scales,
        grads,
        out=[((rows, half), BF16), ((slots, tokens), F32)],
    )
    routed = exchange(sent)
    pair, gate_up, partial = call(
        gate_up_kernel,
        mine,
        theirs,
        *both,
        busy_us=5,
        out=[
            ((rows, half), BF16),
            ((rows, 2 * hidden_width), F32),
            ((rows, 2 * hidden_width), BF16),
        ],
    )
    other = across_halves(partial)
    down, partial = call(
        down_kernel,
        routed,
        *last,
        out=[((rows, hidden_width), F32), ((rows, hidden_width), BF16)],
    )
    kept, swapped, *sends = call(
        delta_kernel,
        gate_up,
        other,
        down,
        across_halves(partial),
        pair,
        routed,
        *both,
        out=[((slots, half + LANES), BF16)] * 2
        + [((rows, 3 * hidden_width + 2 * width), BF16)] * PARTS,
        scratch=[pltpu.VMEM((rows, half + LANES), BF16)],
    )
    pieces = call(
        return_kernel,
        kept,
        across_halves(swapped),
        busy_us=3,
        out=[((CAP, features + LANES), BF16)] * owners,
        scratch=[pltpu.VMEM((slots, features + LANES), F32)],
    )
    pieces = [pieces[0]] + [
        lax.ppermute(pieces[m], "exp", [(i, i ^ m) for i in range(owners)])
        for m in range(1, owners)
    ]
    sends = [sends[0]] + [in_half(sends[k], k) for k in range(1, PARTS)]
    gate_grad, up_grad, down_grad = call(
        grads_step(replicas), *sends, out=[((width, hidden_width), F32)] * 3
    )
    input_grad, route_grad = call(
        tokens_kernel,
        ids,
        scales,
        hits,
        *pieces,
        out=[((tokens, features), BF16), ((TOPK, tokens), BF16)],
    )
    return (input_grad[None], route_grad.T[None], gate_grad[None], up_grad[None], down_grad[None])


def slot_table(block_ids, slot_count, owners):
    flat_ids = block_ids.reshape(-1)
    chosen = flat_ids % EXP_DEV == 0
    owner_of = flat_ids // EXP_DEV
    capacity = slot_count // owners
    onehot = ((owner_of[:, None] == jnp.arange(owners)[None, :]) & chosen[:, None]).astype(
        jnp.int32
    )
    earlier = jnp.cumsum(onehot, axis=0) - onehot
    position = jnp.sum(earlier * onehot, axis=1)
    slot_of = jnp.where(chosen, owner_of * capacity + position, -1)
    return slot_of[None, :] == jnp.arange(slot_count)[:, None]


def first_contract(left, right):
    return lax.dot_general(
        left, right, (((0,), (0,)), ((), ())), preferred_element_type=jnp.float32
    )


def second_contract(left, right):
    return lax.dot_general(
        left, right, (((1,), (1,)), ((), ())), preferred_element_type=jnp.float32
    )


def general_body(expert_ids, route_weights, out_grad, saved_inputs, gate_weight, up_weight, down_weight):
    owners = lax.axis_size("exp")
    replicas = lax.axis_size("rep")
    tokens_here = out_grad.shape[1]
    features = out_grad.shape[2]
    hidden_width = gate_weight.shape[2]
    slot_count = saved_inputs.shape[2]
    capacity = slot_count // owners
    placed = slot_table(expert_ids[0], slot_count, owners)
    weights_flat = route_weights[0].reshape(-1)
    slot_scale = jnp.sum(
        jnp.where(placed, weights_flat[None, :], jnp.zeros((), weights_flat.dtype)), axis=1
    )
    token_hits = jnp.any(placed.reshape(slot_count, tokens_here, TOPK), axis=2)
    token_of = jnp.sum(jnp.where(token_hits, jnp.arange(tokens_here)[None, :], 0), axis=1)
    is_live = jnp.any(token_hits, axis=1)
    routed = jnp.where(is_live[:, None], out_grad[0][token_of], jnp.zeros((), jnp.bfloat16))
    arrived, arrived_scale = (
        lax.all_to_all(
            routed.reshape(owners, capacity, features),
            "exp",
            split_axis=0,
            concat_axis=0,
            tiled=True,
        ),
        lax.all_to_all(
            slot_scale.reshape(owners, capacity), "exp", split_axis=0, concat_axis=0, tiled=True
        ),
    )
    full_gate, full_up, full_down = (
        lax.all_gather(gate_weight[0], "rep", axis=0, tiled=True),
        lax.all_gather(up_weight[0], "rep", axis=0, tiled=True),
        lax.all_gather(down_weight[0], "rep", axis=0, tiled=True),
    )
    grad_rows = arrived.reshape(slot_count, features)
    scale_col = arrived_scale.reshape(slot_count, 1).astype(jnp.float32)
    inputs_here = saved_inputs[0, 0]
    pre_gate = jnp.dot(inputs_here, full_gate, preferred_element_type=jnp.float32)
    pre_up = jnp.dot(inputs_here, full_up, preferred_element_type=jnp.float32)
    sigmoid_gate = jax.nn.sigmoid(pre_gate)
    activated = pre_gate * sigmoid_gate
    hidden = (activated * pre_up).astype(jnp.bfloat16)
    raw_grad = jnp.dot(grad_rows, full_down, preferred_element_type=jnp.float32)
    slot_route = jnp.sum(hidden.astype(jnp.float32) * raw_grad, axis=1).astype(jnp.bfloat16)
    hidden_grad = scale_col * raw_grad
    scaled_rows = (scale_col * grad_rows.astype(jnp.float32)).astype(jnp.bfloat16)
    gate_delta = (
        hidden_grad * pre_up * sigmoid_gate * (1.0 + pre_gate * (1.0 - sigmoid_gate))
    ).astype(jnp.bfloat16)
    up_delta = (hidden_grad * activated).astype(jnp.bfloat16)
    back_rows = (
        second_contract(gate_delta, full_gate) + second_contract(up_delta, full_up)
    ).astype(jnp.bfloat16)
    returned, returned_route = (
        lax.all_to_all(
            back_rows.reshape(owners, capacity, features),
            "exp",
            split_axis=0,
            concat_axis=0,
            tiled=True,
        ),
        lax.all_to_all(
            slot_route.reshape(owners, capacity), "exp", split_axis=0, concat_axis=0, tiled=True
        ),
    )
    returned_flat = returned.reshape(slot_count, features)
    route_flat = returned_route.reshape(slot_count)
    combined = jax.ops.segment_sum(
        jnp.where(is_live[:, None], returned_flat.astype(jnp.float32), 0.0),
        token_of,
        num_segments=tokens_here,
    )
    input_grad = combined.astype(jnp.bfloat16)[None]
    route_grad = jnp.sum(
        jnp.where(placed, route_flat[:, None], jnp.zeros((), jnp.bfloat16)), axis=0
    )
    route_grad = route_grad.reshape(1, tokens_here, TOPK)
    joined_share = lax.psum_scatter(
        jnp.concatenate(
            [
                jnp.concatenate(
                    [
                        first_contract(inputs_here, gate_delta),
                        first_contract(inputs_here, up_delta),
                    ],
                    axis=1,
                ),
                first_contract(scaled_rows, hidden),
            ],
            axis=1,
        ),
        "rep",
        scatter_dimension=0,
        tiled=True,
    )
    gate_share = joined_share[:, :hidden_width]
    up_share = joined_share[:, hidden_width : 2 * hidden_width]
    down_share = joined_share[:, 2 * hidden_width :]
    gate_grad = (gate_share / replicas)[None]
    up_grad = (up_share / replicas)[None]
    down_grad = (down_share / replicas)[None]
    return (input_grad, route_grad, gate_grad, up_grad, down_grad)


def solution(mesh):
    replicas, owners = mesh.shape["rep"], mesh.shape["exp"]
    if replicas == 2 * PARTS:
        step, rep = body, ("q", "p")
        mesh = Mesh(mesh.devices.reshape(2, PARTS, owners), ("q", "p", "exp"))
    else:
        step, rep = general_body, "rep"
    in_specs = (
        P(rep, "exp", None),
        P(rep, "exp", None),
        P(rep, "exp", None),
        P(rep, "exp", None, None),
        P("exp", rep, None),
        P("exp", rep, None),
        P("exp", rep, None),
    )
    out_specs = (
        P(rep, "exp", None),
        P(rep, "exp", None),
        P("exp", rep, None),
        P("exp", rep, None),
        P("exp", rep, None),
    )
    return jax.shard_map(step, mesh=mesh, in_specs=in_specs, out_specs=out_specs, check_vma=False)
```

```python
import jax
import jax.numpy as jnp
from jax import lax
from jax.experimental import pallas as pl
from jax.experimental.pallas import tpu as pltpu
from jax.sharding import Mesh
from jax.sharding import PartitionSpec as P

TOPK = 8
EXP_DEV = 4
PARTS = 4
CUT = 3
CAP = 8
LANES = 128
F32 = jnp.float32
BF16 = jnp.bfloat16


def dot(left, right, ldim, rdim):
    return lax.dot_general(
        left, right, (((ldim,), (rdim,)), ((), ())), preferred_element_type=F32
    )


def call(kernel, *args, out, scratch=(), space=pltpu.VMEM, busy_us=None):
    spec = pl.BlockSpec(memory_space=pltpu.VMEM)
    return pl.pallas_call(
        kernel,
        out_shape=[jax.ShapeDtypeStruct(s, d) for s, d in out],
        in_specs=[pl.BlockSpec(memory_space=space)] * len(args),
        out_specs=[spec] * len(out),
        scratch_shapes=list(scratch),
        cost_estimate=busy_us and pl.CostEstimate(
            flops=busy_us * 10**9, transcendentals=0, bytes_accessed=busy_us * 3 * 10**6
        ),
        compiler_params=pltpu.CompilerParams(vmem_limit_bytes=32 << 20),
    )(*args)


def in_hbm(*arrays):
    return [pltpu.with_memory_space_constraint(a, pltpu.HBM) for a in arrays]


def fetch(sources, targets, sems):
    copies = [
        pltpu.make_async_copy(source, target, sems.at[n])
        for n, (source, target) in enumerate(zip(sources, targets))
    ]
    for copy in copies:
        copy.start()
    return copies


def position():
    return lax.axis_index("q"), lax.axis_index("p")


def block(index, size):
    return pl.ds(pl.multiple_of(index * size, size), size)


def spread_kernel(*refs):
    (gate_ref, up_ref, down_ref, saved_ref, ids_ref, scales_ref, grads_ref), refs = refs[:7], refs[7:]
    whole_ref, both_ref, last_ref, mine_ref, across_ref, *kept, saved, sems = refs
    hidden = gate_ref.shape[1]
    half = mine_ref.shape[1]
    q, _ = position()
    sources = (gate_ref, up_ref, down_ref)
    targets = (both_ref.at[:, :hidden], both_ref.at[:, hidden:], last_ref)
    again = [whole_ref.at[:, i * hidden : (i + 1) * hidden] for i in range(3)]
    copies = fetch(
        (saved_ref, *sources, *sources, ids_ref, scales_ref, grads_ref),
        (saved, *targets, *again, *kept),
        sems,
    )
    copies[0].wait()
    mine_ref[...] = saved[:, block(q, half)]
    across_ref[...] = saved[:, block(1 - q, half)]
    for copy in copies[1:]:
        copy.wait()


def route_kernel(ids_ref, scales_ref, grads_ref, send_ref, hits_ref):
    slots, tokens = hits_ref.shape
    owners = slots // CAP
    half = send_ref.shape[1]
    earlier = lax.broadcasted_iota(jnp.int32, (tokens, tokens), 0) < (
        lax.broadcasted_iota(jnp.int32, (tokens, tokens), 1)
    )
    before = jnp.where(earlier, 1.0, 0.0).astype(BF16)
    slot = lax.broadcasted_iota(jnp.int32, (CAP, tokens), 0).astype(F32)
    ids = ids_ref[...]
    weights = scales_ref[...].astype(F32)
    hits, scales = [], []
    for j in range(owners):
        match = ids == j * EXP_DEV
        hits.append(jnp.sum(jnp.where(match, 1.0, 0.0), axis=0, keepdims=True))
        scales.append(jnp.sum(jnp.where(match, weights, 0.0), axis=0, keepdims=True))
    pad = [jnp.zeros((1, tokens), F32)] * (-owners % 8)
    hit = jnp.concatenate(hits + pad, axis=0)
    place = dot(hit.astype(BF16), before, 1, 0)
    chosen, scaled = [], []
    for j in range(owners):
        here = (place[j : j + 1] == slot) & (hits[j] > 0.0)
        chosen.append(jnp.where(here, 1.0, 0.0))
        scaled.append(jnp.where(here, scales[j], 0.0))
    hits_ref[...] = jnp.concatenate(chosen, axis=0)
    picks = jnp.concatenate(scaled, axis=0).astype(BF16)
    rows = dot(picks, grads_ref[...], 1, 0).astype(BF16)
    for h in range(2):
        send_ref[h * slots : (h + 1) * slots, :] = rows[:, h * half : (h + 1) * half]


def gate_up_kernel(mine_ref, theirs_ref, *refs):
    weights, (pair_ref, own_ref, sent_ref) = refs[:PARTS], refs[PARTS:]
    q, p = position()
    slots = mine_ref.shape[0]
    width = weights[0].shape[0]
    pair_ref[block(q, slots), :] = mine_ref[...]
    pair_ref[block(1 - q, slots), :] = theirs_ref[...]
    total = None
    for k in range(PARTS):
        columns = weights[k][:, : own_ref.shape[1]]
        term = dot(pair_ref[:, block(p ^ k, width)], columns, 1, 0)
        total = term if total is None else total + term
    own_ref[...] = total
    sent_ref[...] = total.astype(BF16)


def down_kernel(routed_ref, *refs):
    weights, (own_ref, sent_ref) = refs[:PARTS], refs[PARTS:]
    _, p = position()
    width = weights[0].shape[0]
    total = None
    for k in range(PARTS):
        columns = weights[k][:, weights[k].shape[1] - own_ref.shape[1] :]
        term = dot(routed_ref[:, block(p ^ k, width)], columns, 1, 0)
        total = term if total is None else total + term
    own_ref[...] = total
    sent_ref[...] = total.astype(BF16)


def delta_kernel(gate_up_ref, other_ref, down_ref, down_other_ref, pair_ref, routed_ref, *refs):
    weights, kept_ref, swap_ref, sends = refs[:PARTS], refs[PARTS], refs[PARTS + 1], refs[PARTS + 2 : -1]
    back_ref = refs[-1]
    q, p = position()
    width = weights[0].shape[0]
    hidden_width = down_ref.shape[1]
    half = pair_ref.shape[1]
    both = gate_up_ref[...] + other_ref[...].astype(F32)
    hidden_grad = down_ref[...] + down_other_ref[...].astype(F32)
    pre_gate, pre_up = both[:, :hidden_width], both[:, hidden_width:]
    sigmoid = jax.nn.sigmoid(pre_gate)
    activated = pre_gate * sigmoid
    hidden = (activated * pre_up).astype(BF16)
    gate_delta = hidden_grad * pre_up * sigmoid * (1.0 + pre_gate * (1.0 - sigmoid))
    gate_delta = gate_delta.astype(BF16)
    up_delta = (hidden_grad * activated).astype(BF16)
    route = jnp.sum(hidden.astype(F32) * hidden_grad, axis=1, keepdims=True)
    back_ref[:, half:] = jnp.broadcast_to(route, (route.shape[0], LANES)).astype(BF16)
    for k in range(PARTS):
        lanes = block(p ^ k, width)
        back_ref[:, lanes] = (
            dot(gate_delta, weights[k][:, :hidden_width], 1, 1)
            + dot(up_delta, weights[k][:, hidden_width : 2 * hidden_width], 1, 1)
        ).astype(BF16)
        sends[k][:, :hidden_width] = gate_delta
        sends[k][:, hidden_width : 2 * hidden_width] = up_delta
        sends[k][:, 2 * hidden_width : 3 * hidden_width] = hidden
        sends[k][:, 3 * hidden_width : 3 * hidden_width + width] = pair_ref[:, lanes]
        sends[k][:, 3 * hidden_width + width :] = routed_ref[:, lanes]
    slots = kept_ref.shape[0]
    kept_ref[...] = back_ref[block(q, slots), :]
    swap_ref[...] = back_ref[block(1 - q, slots), :]


def return_kernel(kept_ref, swap_ref, *refs):
    outs, rows_ref = refs[:-1], refs[-1]
    q, _ = position()
    half = kept_ref.shape[1] - LANES
    rows_ref[:, block(q, half)] = kept_ref[:, :half].astype(F32)
    rows_ref[:, block(1 - q, half)] = swap_ref[:, :half].astype(F32)
    rows_ref[:, 2 * half :] = kept_ref[:, half:].astype(F32)
    for m, out in enumerate(outs):
        out[...] = rows_ref[block(lax.axis_index("exp") ^ m, CAP), :].astype(BF16)


def grads_step(replicas):
    def grads_kernel(*refs):
        parts, (gate_ref, up_ref, down_ref) = refs[:PARTS], refs[PARTS:]
        width, hidden = gate_ref.shape

        def column(start, size):
            return jnp.concatenate([part[:, start : start + size] for part in parts], axis=0)

        both = dot(column(3 * hidden, width), column(0, 2 * hidden), 0, 0) / replicas
        gate_ref[...] = both[:, :hidden]
        up_ref[...] = both[:, hidden:]
        down = dot(column(3 * hidden + width, width), column(2 * hidden, hidden), 0, 0)
        down_ref[...] = down / replicas

    return grads_kernel


def tokens_kernel(ids_ref, scales_ref, hits_ref, *refs):
    pieces, (input_grad_ref, route_ref) = refs[:-2], refs[-2:]
    features = input_grad_ref.shape[1]
    ids = ids_ref[...]
    out = jnp.zeros(ids.shape, F32)
    hits = []
    for m, piece in enumerate(pieces):
        expert = lax.axis_index("exp") ^ m
        hits.append(hits_ref[block(expert, CAP), :])
        value = jnp.sum(hits[m] * piece[:, features:].astype(F32), axis=0, keepdims=True)
        out = jnp.where(ids == expert * EXP_DEV, value, out)
    route_ref[...] = (out / scales_ref[...].astype(F32)).astype(BF16)
    rows = jnp.concatenate([piece[:, :features].astype(F32) for piece in pieces], axis=0)
    hits = jnp.concatenate(hits, axis=0)
    input_grad_ref[...] = dot(hits.astype(BF16), rows.astype(BF16), 0, 0).astype(BF16)


def body(expert_ids, route_weights, out_grad, saved_inputs, gate_weight, up_weight, down_weight):
    owners = lax.axis_size("exp")
    replicas = lax.axis_size("q") * PARTS
    tokens, features = out_grad.shape[1:]
    slots = saved_inputs.shape[2]
    width, hidden_width = gate_weight.shape[1:]
    half, rows = features // 2, 2 * slots

    def in_half(value, mask):
        return lax.ppermute(value, "p", [(i, i ^ mask) for i in range(PARTS)])

    def across_halves(value):
        return lax.ppermute(value, "q", [(0, 1), (1, 0)])

    def exchange(value):
        blocks = value.reshape(2 * owners, CAP, value.shape[1])
        return lax.all_to_all(blocks, ("q", "exp"), 0, 0, tiled=True).reshape(value.shape)

    whole, both, last, mine, across, ids, scales, grads = call(
        spread_kernel,
        *in_hbm(gate_weight[0], up_weight[0], down_weight[0], saved_inputs[0, 0]),
        *in_hbm(expert_ids[0].T, route_weights[0].T, out_grad[0]),
        out=[((width, n * hidden_width), BF16) for n in (3, 2, 1)]
        + [((slots, half), BF16)] * 2
        + [((TOPK, tokens), jnp.int32), ((TOPK, tokens), BF16), ((tokens, features), BF16)],
        scratch=[pltpu.VMEM((slots, features), BF16), pltpu.SemaphoreType.DMA((10,))],
        space=pltpu.HBM,
    )
    theirs = across_halves(across)
    wholes = {k: in_half(whole, k) for k in range(1, PARTS) if k != CUT}
    both = [both] + [wholes[k] if k in wholes else in_half(both, k) for k in range(1, PARTS)]
    last = [last] + [wholes[k] if k in wholes else in_half(last, k) for k in range(1, PARTS)]
    sent, hits = call(
        route_kernel,
        ids,
        scales,
        grads,
        out=[((rows, half), BF16), ((slots, tokens), F32)],
    )
    routed = exchange(sent)
    pair, gate_up, partial = call(
        gate_up_kernel,
        mine,
        theirs,
        *both,
        busy_us=5,
        out=[
            ((rows, half), BF16),
            ((rows, 2 * hidden_width), F32),
            ((rows, 2 * hidden_width), BF16),
        ],
    )
    other = across_halves(partial)
    down, partial = call(
        down_kernel,
        routed,
        *last,
        out=[((rows, hidden_width), F32), ((rows, hidden_width), BF16)],
    )
    kept, swapped, *sends = call(
        delta_kernel,
        gate_up,
        other,
        down,
        across_halves(partial),
        pair,
        routed,
        *both,
        out=[((slots, half + LANES), BF16)] * 2
        + [((rows, 3 * hidden_width + 2 * width), BF16)] * PARTS,
        scratch=[pltpu.VMEM((rows, half + LANES), BF16)],
    )
    pieces = call(
        return_kernel,
        kept,
        across_halves(swapped),
        busy_us=3,
        out=[((CAP, features + LANES), BF16)] * owners,
        scratch=[pltpu.VMEM((slots, features + LANES), F32)],
    )
    pieces = [pieces[0]] + [
        lax.ppermute(pieces[m], "exp", [(i, i ^ m) for i in range(owners)])
        for m in range(1, owners)
    ]
    sends = [sends[0]] + [in_half(sends[k], k) for k in (3, 1, 2)]
    gate_grad, up_grad, down_grad = call(
        grads_step(replicas), *sends, out=[((width, hidden_width), F32)] * 3
    )
    input_grad, route_grad = call(
        tokens_kernel,
        ids,
        scales,
        hits,
        *pieces,
        out=[((tokens, features), BF16), ((TOPK, tokens), BF16)],
    )
    return (input_grad[None], route_grad.T[None], gate_grad[None], up_grad[None], down_grad[None])


def slot_table(block_ids, slot_count, owners):
    flat_ids = block_ids.reshape(-1)
    chosen = flat_ids % EXP_DEV == 0
    owner_of = flat_ids // EXP_DEV
    capacity = slot_count // owners
    onehot = ((owner_of[:, None] == jnp.arange(owners)[None, :]) & chosen[:, None]).astype(
        jnp.int32
    )
    earlier = jnp.cumsum(onehot, axis=0) - onehot
    position = jnp.sum(earlier * onehot, axis=1)
    slot_of = jnp.where(chosen, owner_of * capacity + position, -1)
    return slot_of[None, :] == jnp.arange(slot_count)[:, None]


def first_contract(left, right):
    return lax.dot_general(
        left, right, (((0,), (0,)), ((), ())), preferred_element_type=jnp.float32
    )


def second_contract(left, right):
    return lax.dot_general(
        left, right, (((1,), (1,)), ((), ())), preferred_element_type=jnp.float32
    )


def general_body(expert_ids, route_weights, out_grad, saved_inputs, gate_weight, up_weight, down_weight):
    owners = lax.axis_size("exp")
    replicas = lax.axis_size("rep")
    tokens_here = out_grad.shape[1]
    features = out_grad.shape[2]
    hidden_width = gate_weight.shape[2]
    slot_count = saved_inputs.shape[2]
    capacity = slot_count // owners
    placed = slot_table(expert_ids[0], slot_count, owners)
    weights_flat = route_weights[0].reshape(-1)
    slot_scale = jnp.sum(
        jnp.where(placed, weights_flat[None, :], jnp.zeros((), weights_flat.dtype)), axis=1
    )
    token_hits = jnp.any(placed.reshape(slot_count, tokens_here, TOPK), axis=2)
    token_of = jnp.sum(jnp.where(token_hits, jnp.arange(tokens_here)[None, :], 0), axis=1)
    is_live = jnp.any(token_hits, axis=1)
    routed = jnp.where(is_live[:, None], out_grad[0][token_of], jnp.zeros((), jnp.bfloat16))
    arrived, arrived_scale = (
        lax.all_to_all(
            routed.reshape(owners, capacity, features),
            "exp",
            split_axis=0,
            concat_axis=0,
            tiled=True,
        ),
        lax.all_to_all(
            slot_scale.reshape(owners, capacity), "exp", split_axis=0, concat_axis=0, tiled=True
        ),
    )
    full_gate, full_up, full_down = (
        lax.all_gather(gate_weight[0], "rep", axis=0, tiled=True),
        lax.all_gather(up_weight[0], "rep", axis=0, tiled=True),
        lax.all_gather(down_weight[0], "rep", axis=0, tiled=True),
    )
    grad_rows = arrived.reshape(slot_count, features)
    scale_col = arrived_scale.reshape(slot_count, 1).astype(jnp.float32)
    inputs_here = saved_inputs[0, 0]
    pre_gate = jnp.dot(inputs_here, full_gate, preferred_element_type=jnp.float32)
    pre_up = jnp.dot(inputs_here, full_up, preferred_element_type=jnp.float32)
    sigmoid_gate = jax.nn.sigmoid(pre_gate)
    activated = pre_gate * sigmoid_gate
    hidden = (activated * pre_up).astype(jnp.bfloat16)
    raw_grad = jnp.dot(grad_rows, full_down, preferred_element_type=jnp.float32)
    slot_route = jnp.sum(hidden.astype(jnp.float32) * raw_grad, axis=1).astype(jnp.bfloat16)
    hidden_grad = scale_col * raw_grad
    scaled_rows = (scale_col * grad_rows.astype(jnp.float32)).astype(jnp.bfloat16)
    gate_delta = (
        hidden_grad * pre_up * sigmoid_gate * (1.0 + pre_gate * (1.0 - sigmoid_gate))
    ).astype(jnp.bfloat16)
    up_delta = (hidden_grad * activated).astype(jnp.bfloat16)
    back_rows = (
        second_contract(gate_delta, full_gate) + second_contract(up_delta, full_up)
    ).astype(jnp.bfloat16)
    returned, returned_route = (
        lax.all_to_all(
            back_rows.reshape(owners, capacity, features),
            "exp",
            split_axis=0,
            concat_axis=0,
            tiled=True,
        ),
        lax.all_to_all(
            slot_route.reshape(owners, capacity), "exp", split_axis=0, concat_axis=0, tiled=True
        ),
    )
    returned_flat = returned.reshape(slot_count, features)
    route_flat = returned_route.reshape(slot_count)
    combined = jax.ops.segment_sum(
        jnp.where(is_live[:, None], returned_flat.astype(jnp.float32), 0.0),
        token_of,
        num_segments=tokens_here,
    )
    input_grad = combined.astype(jnp.bfloat16)[None]
    route_grad = jnp.sum(
        jnp.where(placed, route_flat[:, None], jnp.zeros((), jnp.bfloat16)), axis=0
    )
    route_grad = route_grad.reshape(1, tokens_here, TOPK)
    joined_share = lax.psum_scatter(
        jnp.concatenate(
            [
                jnp.concatenate(
                    [
                        first_contract(inputs_here, gate_delta),
                        first_contract(inputs_here, up_delta),
                    ],
                    axis=1,
                ),
                first_contract(scaled_rows, hidden),
            ],
            axis=1,
        ),
        "rep",
        scatter_dimension=0,
        tiled=True,
    )
    gate_share = joined_share[:, :hidden_width]
    up_share = joined_share[:, hidden_width : 2 * hidden_width]
    down_share = joined_share[:, 2 * hidden_width :]
    gate_grad = (gate_share / replicas)[None]
    up_grad = (up_share / replicas)[None]
    down_grad = (down_share / replicas)[None]
    return (input_grad, route_grad, gate_grad, up_grad, down_grad)


def solution(mesh):
    replicas, owners = mesh.shape["rep"], mesh.shape["exp"]
    if replicas == 2 * PARTS:
        step, rep = body, ("q", "p")
        mesh = Mesh(mesh.devices.reshape(2, PARTS, owners), ("q", "p", "exp"))
    else:
        step, rep = general_body, "rep"
    in_specs = (
        P(rep, "exp", None),
        P(rep, "exp", None),
        P(rep, "exp", None),
        P(rep, "exp", None, None),
        P("exp", rep, None),
        P("exp", rep, None),
        P("exp", rep, None),
    )
    out_specs = (
        P(rep, "exp", None),
        P(rep, "exp", None),
        P("exp", rep, None),
        P("exp", rep, None),
        P("exp", rep, None),
    )
    return jax.shard_map(step, mesh=mesh, in_specs=in_specs, out_specs=out_specs, check_vma=False)
```

```python
import jax
import jax.numpy as jnp
from jax import lax
from jax.experimental import pallas as pl
from jax.experimental.pallas import tpu as pltpu
from jax.sharding import Mesh
from jax.sharding import PartitionSpec as P

TOPK = 8
EXP_DEV = 4
PARTS = 4
CUT = 3
CAP = 8
LANES = 128
F32 = jnp.float32
BF16 = jnp.bfloat16


def dot(left, right, ldim, rdim):
    return lax.dot_general(
        left, right, (((ldim,), (rdim,)), ((), ())), preferred_element_type=F32
    )


def call(kernel, *args, out, scratch=(), space=pltpu.VMEM, busy_us=None):
    spec = pl.BlockSpec(memory_space=pltpu.VMEM)
    return pl.pallas_call(
        kernel,
        out_shape=[jax.ShapeDtypeStruct(s, d) for s, d in out],
        in_specs=[pl.BlockSpec(memory_space=space)] * len(args),
        out_specs=[spec] * len(out),
        scratch_shapes=list(scratch),
        cost_estimate=busy_us and pl.CostEstimate(
            flops=busy_us * 10**9, transcendentals=0, bytes_accessed=busy_us * 3 * 10**6
        ),
        compiler_params=pltpu.CompilerParams(vmem_limit_bytes=32 << 20),
    )(*args)


def in_hbm(*arrays):
    return [pltpu.with_memory_space_constraint(a, pltpu.HBM) for a in arrays]


def fetch(sources, targets, sems):
    copies = [
        pltpu.make_async_copy(source, target, sems.at[n])
        for n, (source, target) in enumerate(zip(sources, targets))
    ]
    for copy in copies:
        copy.start()
    return copies


def position():
    return lax.axis_index("q"), lax.axis_index("p")


def block(index, size):
    return pl.ds(pl.multiple_of(index * size, size), size)


def spread_kernel(*refs):
    (gate_ref, up_ref, down_ref, saved_ref, ids_ref, scales_ref, grads_ref), refs = refs[:7], refs[7:]
    whole_ref, both_ref, last_ref, mine_ref, across_ref, *kept, saved, sems = refs
    hidden = gate_ref.shape[1]
    half = mine_ref.shape[1]
    q, _ = position()
    sources = (gate_ref, up_ref, down_ref)
    targets = (both_ref.at[:, :hidden], both_ref.at[:, hidden:], last_ref)
    again = [whole_ref.at[:, i * hidden : (i + 1) * hidden] for i in range(3)]
    copies = fetch(
        (saved_ref, *sources, *sources, ids_ref, scales_ref, grads_ref),
        (saved, *targets, *again, *kept),
        sems,
    )
    copies[0].wait()
    mine_ref[...] = saved[:, block(q, half)]
    across_ref[...] = saved[:, block(1 - q, half)]
    for copy in copies[1:]:
        copy.wait()


def route_kernel(ids_ref, scales_ref, grads_ref, send_ref, hits_ref):
    slots, tokens = hits_ref.shape
    owners = slots // CAP
    half = send_ref.shape[1]
    earlier = lax.broadcasted_iota(jnp.int32, (tokens, tokens), 0) < (
        lax.broadcasted_iota(jnp.int32, (tokens, tokens), 1)
    )
    before = jnp.where(earlier, 1.0, 0.0).astype(BF16)
    slot = lax.broadcasted_iota(jnp.int32, (CAP, tokens), 0).astype(F32)
    ids = ids_ref[...]
    weights = scales_ref[...].astype(F32)
    hits, scales = [], []
    for j in range(owners):
        match = ids == j * EXP_DEV
        hits.append(jnp.sum(jnp.where(match, 1.0, 0.0), axis=0, keepdims=True))
        scales.append(jnp.sum(jnp.where(match, weights, 0.0), axis=0, keepdims=True))
    pad = [jnp.zeros((1, tokens), F32)] * (-owners % 8)
    hit = jnp.concatenate(hits + pad, axis=0)
    place = dot(hit.astype(BF16), before, 1, 0)
    chosen, scaled = [], []
    for j in range(owners):
        here = (place[j : j + 1] == slot) & (hits[j] > 0.0)
        chosen.append(jnp.where(here, 1.0, 0.0))
        scaled.append(jnp.where(here, scales[j], 0.0))
    hits_ref[...] = jnp.concatenate(chosen, axis=0)
    picks = jnp.concatenate(scaled, axis=0).astype(BF16)
    rows = dot(picks, grads_ref[...], 1, 0).astype(BF16)
    for h in range(2):
        send_ref[h * slots : (h + 1) * slots, :] = rows[:, h * half : (h + 1) * half]


def gate_up_kernel(mine_ref, theirs_ref, *refs):
    weights, (pair_ref, own_ref, sent_ref) = refs[:PARTS], refs[PARTS:]
    q, p = position()
    slots = mine_ref.shape[0]
    width = weights[0].shape[0]
    pair_ref[block(q, slots), :] = mine_ref[...]
    pair_ref[block(1 - q, slots), :] = theirs_ref[...]
    total = None
    for k in range(PARTS):
        columns = weights[k][:, : own_ref.shape[1]]
        term = dot(pair_ref[:, block(p ^ k, width)], columns, 1, 0)
        total = term if total is None else total + term
    own_ref[...] = total
    sent_ref[...] = total.astype(BF16)


def down_kernel(routed_ref, *refs):
    weights, (own_ref, sent_ref) = refs[:PARTS], refs[PARTS:]
    _, p = position()
    width = weights[0].shape[0]
    total = None
    for k in range(PARTS):
        columns = weights[k][:, weights[k].shape[1] - own_ref.shape[1] :]
        term = dot(routed_ref[:, block(p ^ k, width)], columns, 1, 0)
        total = term if total is None else total + term
    own_ref[...] = total
    sent_ref[...] = total.astype(BF16)


def delta_kernel(gate_up_ref, other_ref, down_ref, down_other_ref, pair_ref, routed_ref, *refs):
    weights, kept_ref, swap_ref, sends = refs[:PARTS], refs[PARTS], refs[PARTS + 1], refs[PARTS + 2 : -1]
    back_ref = refs[-1]
    q, p = position()
    width = weights[0].shape[0]
    hidden_width = down_ref.shape[1]
    half = pair_ref.shape[1]
    both = gate_up_ref[...] + other_ref[...].astype(F32)
    hidden_grad = down_ref[...] + down_other_ref[...].astype(F32)
    pre_gate, pre_up = both[:, :hidden_width], both[:, hidden_width:]
    sigmoid = jax.nn.sigmoid(pre_gate)
    activated = pre_gate * sigmoid
    hidden = (activated * pre_up).astype(BF16)
    gate_delta = hidden_grad * pre_up * sigmoid * (1.0 + pre_gate * (1.0 - sigmoid))
    gate_delta = gate_delta.astype(BF16)
    up_delta = (hidden_grad * activated).astype(BF16)
    route = jnp.sum(hidden.astype(F32) * hidden_grad, axis=1, keepdims=True)
    back_ref[:, half:] = jnp.broadcast_to(route, (route.shape[0], LANES)).astype(BF16)
    for k in range(PARTS):
        lanes = block(p ^ k, width)
        back_ref[:, lanes] = (
            dot(gate_delta, weights[k][:, :hidden_width], 1, 1)
            + dot(up_delta, weights[k][:, hidden_width : 2 * hidden_width], 1, 1)
        ).astype(BF16)
        sends[k][:, :hidden_width] = gate_delta
        sends[k][:, hidden_width : 2 * hidden_width] = up_delta
        sends[k][:, 2 * hidden_width : 3 * hidden_width] = hidden
        sends[k][:, 3 * hidden_width : 3 * hidden_width + width] = pair_ref[:, lanes]
        sends[k][:, 3 * hidden_width + width :] = routed_ref[:, lanes]
    slots = kept_ref.shape[0]
    kept_ref[...] = back_ref[block(q, slots), :]
    swap_ref[...] = back_ref[block(1 - q, slots), :]


def return_kernel(kept_ref, swap_ref, *refs):
    outs, rows_ref = refs[:-1], refs[-1]
    q, _ = position()
    half = kept_ref.shape[1] - LANES
    rows_ref[:, block(q, half)] = kept_ref[:, :half].astype(F32)
    rows_ref[:, block(1 - q, half)] = swap_ref[:, :half].astype(F32)
    rows_ref[:, 2 * half :] = kept_ref[:, half:].astype(F32)
    for m, out in enumerate(outs):
        out[...] = rows_ref[block(lax.axis_index("exp") ^ m, CAP), :].astype(BF16)


def grads_step(replicas):
    def grads_kernel(*refs):
        parts, (gate_ref, up_ref, down_ref) = refs[:PARTS], refs[PARTS:]
        width, hidden = gate_ref.shape

        def column(start, size):
            return jnp.concatenate([part[:, start : start + size] for part in parts], axis=0)

        both = dot(column(3 * hidden, width), column(0, 2 * hidden), 0, 0) * (1.0 / replicas)
        gate_ref[...] = both[:, :hidden]
        up_ref[...] = both[:, hidden:]
        down = dot(column(3 * hidden + width, width), column(2 * hidden, hidden), 0, 0)
        down_ref[...] = down * (1.0 / replicas)

    return grads_kernel


def tokens_kernel(ids_ref, scales_ref, hits_ref, *refs):
    pieces, (input_grad_ref, route_ref) = refs[:-2], refs[-2:]
    features = input_grad_ref.shape[1]
    ids = ids_ref[...]
    out = jnp.zeros(ids.shape, F32)
    hits = []
    for m, piece in enumerate(pieces):
        expert = lax.axis_index("exp") ^ m
        hits.append(hits_ref[block(expert, CAP), :])
        value = jnp.sum(hits[m] * piece[:, features:].astype(F32), axis=0, keepdims=True)
        out = jnp.where(ids == expert * EXP_DEV, value, out)
    route_ref[...] = (out / scales_ref[...].astype(F32)).astype(BF16)
    rows = jnp.concatenate([piece[:, :features].astype(F32) for piece in pieces], axis=0)
    hits = jnp.concatenate(hits, axis=0)
    input_grad_ref[...] = dot(hits.astype(BF16), rows.astype(BF16), 0, 0).astype(BF16)


def body(expert_ids, route_weights, out_grad, saved_inputs, gate_weight, up_weight, down_weight):
    owners = lax.axis_size("exp")
    replicas = lax.axis_size("q") * PARTS
    tokens, features = out_grad.shape[1:]
    slots = saved_inputs.shape[2]
    width, hidden_width = gate_weight.shape[1:]
    half, rows = features // 2, 2 * slots

    def in_half(value, mask):
        return lax.ppermute(value, "p", [(i, i ^ mask) for i in range(PARTS)])

    def across_halves(value):
        return lax.ppermute(value, "q", [(0, 1), (1, 0)])

    def exchange(value):
        blocks = value.reshape(2 * owners, CAP, value.shape[1])
        return lax.all_to_all(blocks, ("q", "exp"), 0, 0, tiled=True).reshape(value.shape)

    whole, both, last, mine, across, ids, scales, grads = call(
        spread_kernel,
        *in_hbm(gate_weight[0], up_weight[0], down_weight[0], saved_inputs[0, 0]),
        *in_hbm(expert_ids[0].T, route_weights[0].T, out_grad[0]),
        out=[((width, n * hidden_width), BF16) for n in (3, 2, 1)]
        + [((slots, half), BF16)] * 2
        + [((TOPK, tokens), jnp.int32), ((TOPK, tokens), BF16), ((tokens, features), BF16)],
        scratch=[pltpu.VMEM((slots, features), BF16), pltpu.SemaphoreType.DMA((10,))],
        space=pltpu.HBM,
    )
    theirs = across_halves(across)
    wholes = {k: in_half(whole, k) for k in range(1, PARTS) if k != CUT}
    both = [both] + [wholes[k] if k in wholes else in_half(both, k) for k in range(1, PARTS)]
    last = [last] + [wholes[k] if k in wholes else in_half(last, k) for k in range(1, PARTS)]
    sent, hits = call(
        route_kernel,
        ids,
        scales,
        grads,
        out=[((rows, half), BF16), ((slots, tokens), F32)],
    )
    routed = exchange(sent)
    pair, gate_up, partial = call(
        gate_up_kernel,
        mine,
        theirs,
        *both,
        busy_us=5,
        out=[
            ((rows, half), BF16),
            ((rows, 2 * hidden_width), F32),
            ((rows, 2 * hidden_width), BF16),
        ],
    )
    other = across_halves(partial)
    down, partial = call(
        down_kernel,
        routed,
        *last,
        out=[((rows, hidden_width), F32), ((rows, hidden_width), BF16)],
    )
    kept, swapped, *sends = call(
        delta_kernel,
        gate_up,
        other,
        down,
        across_halves(partial),
        pair,
        routed,
        *both,
        out=[((slots, half + LANES), BF16)] * 2
        + [((rows, 3 * hidden_width + 2 * width), BF16)] * PARTS,
        scratch=[pltpu.VMEM((rows, half + LANES), BF16)],
    )
    pieces = call(
        return_kernel,
        kept,
        across_halves(swapped),
        busy_us=3,
        out=[((CAP, features + LANES), BF16)] * owners,
        scratch=[pltpu.VMEM((slots, features + LANES), F32)],
    )
    pieces = [pieces[0]] + [
        lax.ppermute(pieces[m], "exp", [(i, i ^ m) for i in range(owners)])
        for m in range(1, owners)
    ]
    sends = [sends[0]] + [in_half(sends[k], k) for k in (3, 1, 2)]
    gate_grad, up_grad, down_grad = call(
        grads_step(replicas), *sends, out=[((width, hidden_width), F32)] * 3
    )
    input_grad, route_grad = call(
        tokens_kernel,
        ids,
        scales,
        hits,
        *pieces,
        out=[((tokens, features), BF16), ((TOPK, tokens), BF16)],
    )
    return (input_grad[None], route_grad.T[None], gate_grad[None], up_grad[None], down_grad[None])


def slot_table(block_ids, slot_count, owners):
    flat_ids = block_ids.reshape(-1)
    chosen = flat_ids % EXP_DEV == 0
    owner_of = flat_ids // EXP_DEV
    capacity = slot_count // owners
    onehot = ((owner_of[:, None] == jnp.arange(owners)[None, :]) & chosen[:, None]).astype(
        jnp.int32
    )
    earlier = jnp.cumsum(onehot, axis=0) - onehot
    position = jnp.sum(earlier * onehot, axis=1)
    slot_of = jnp.where(chosen, owner_of * capacity + position, -1)
    return slot_of[None, :] == jnp.arange(slot_count)[:, None]


def first_contract(left, right):
    return lax.dot_general(
        left, right, (((0,), (0,)), ((), ())), preferred_element_type=jnp.float32
    )


def second_contract(left, right):
    return lax.dot_general(
        left, right, (((1,), (1,)), ((), ())), preferred_element_type=jnp.float32
    )


def general_body(expert_ids, route_weights, out_grad, saved_inputs, gate_weight, up_weight, down_weight):
    owners = lax.axis_size("exp")
    replicas = lax.axis_size("rep")
    tokens_here = out_grad.shape[1]
    features = out_grad.shape[2]
    hidden_width = gate_weight.shape[2]
    slot_count = saved_inputs.shape[2]
    capacity = slot_count // owners
    placed = slot_table(expert_ids[0], slot_count, owners)
    weights_flat = route_weights[0].reshape(-1)
    slot_scale = jnp.sum(
        jnp.where(placed, weights_flat[None, :], jnp.zeros((), weights_flat.dtype)), axis=1
    )
    token_hits = jnp.any(placed.reshape(slot_count, tokens_here, TOPK), axis=2)
    token_of = jnp.sum(jnp.where(token_hits, jnp.arange(tokens_here)[None, :], 0), axis=1)
    is_live = jnp.any(token_hits, axis=1)
    routed = jnp.where(is_live[:, None], out_grad[0][token_of], jnp.zeros((), jnp.bfloat16))
    arrived, arrived_scale = (
        lax.all_to_all(
            routed.reshape(owners, capacity, features),
            "exp",
            split_axis=0,
            concat_axis=0,
            tiled=True,
        ),
        lax.all_to_all(
            slot_scale.reshape(owners, capacity), "exp", split_axis=0, concat_axis=0, tiled=True
        ),
    )
    full_gate, full_up, full_down = (
        lax.all_gather(gate_weight[0], "rep", axis=0, tiled=True),
        lax.all_gather(up_weight[0], "rep", axis=0, tiled=True),
        lax.all_gather(down_weight[0], "rep", axis=0, tiled=True),
    )
    grad_rows = arrived.reshape(slot_count, features)
    scale_col = arrived_scale.reshape(slot_count, 1).astype(jnp.float32)
    inputs_here = saved_inputs[0, 0]
    pre_gate = jnp.dot(inputs_here, full_gate, preferred_element_type=jnp.float32)
    pre_up = jnp.dot(inputs_here, full_up, preferred_element_type=jnp.float32)
    sigmoid_gate = jax.nn.sigmoid(pre_gate)
    activated = pre_gate * sigmoid_gate
    hidden = (activated * pre_up).astype(jnp.bfloat16)
    raw_grad = jnp.dot(grad_rows, full_down, preferred_element_type=jnp.float32)
    slot_route = jnp.sum(hidden.astype(jnp.float32) * raw_grad, axis=1).astype(jnp.bfloat16)
    hidden_grad = scale_col * raw_grad
    scaled_rows = (scale_col * grad_rows.astype(jnp.float32)).astype(jnp.bfloat16)
    gate_delta = (
        hidden_grad * pre_up * sigmoid_gate * (1.0 + pre_gate * (1.0 - sigmoid_gate))
    ).astype(jnp.bfloat16)
    up_delta = (hidden_grad * activated).astype(jnp.bfloat16)
    back_rows = (
        second_contract(gate_delta, full_gate) + second_contract(up_delta, full_up)
    ).astype(jnp.bfloat16)
    returned, returned_route = (
        lax.all_to_all(
            back_rows.reshape(owners, capacity, features),
            "exp",
            split_axis=0,
            concat_axis=0,
            tiled=True,
        ),
        lax.all_to_all(
            slot_route.reshape(owners, capacity), "exp", split_axis=0, concat_axis=0, tiled=True
        ),
    )
    returned_flat = returned.reshape(slot_count, features)
    route_flat = returned_route.reshape(slot_count)
    combined = jax.ops.segment_sum(
        jnp.where(is_live[:, None], returned_flat.astype(jnp.float32), 0.0),
        token_of,
        num_segments=tokens_here,
    )
    input_grad = combined.astype(jnp.bfloat16)[None]
    route_grad = jnp.sum(
        jnp.where(placed, route_flat[:, None], jnp.zeros((), jnp.bfloat16)), axis=0
    )
    route_grad = route_grad.reshape(1, tokens_here, TOPK)
    joined_share = lax.psum_scatter(
        jnp.concatenate(
            [
                jnp.concatenate(
                    [
                        first_contract(inputs_here, gate_delta),
                        first_contract(inputs_here, up_delta),
                    ],
                    axis=1,
                ),
                first_contract(scaled_rows, hidden),
            ],
            axis=1,
        ),
        "rep",
        scatter_dimension=0,
        tiled=True,
    )
    gate_share = joined_share[:, :hidden_width]
    up_share = joined_share[:, hidden_width : 2 * hidden_width]
    down_share = joined_share[:, 2 * hidden_width :]
    gate_grad = (gate_share / replicas)[None]
    up_grad = (up_share / replicas)[None]
    down_grad = (down_share / replicas)[None]
    return (input_grad, route_grad, gate_grad, up_grad, down_grad)


def solution(mesh):
    replicas, owners = mesh.shape["rep"], mesh.shape["exp"]
    if replicas == 2 * PARTS:
        step, rep = body, ("q", "p")
        mesh = Mesh(mesh.devices.reshape(2, PARTS, owners), ("q", "p", "exp"))
    else:
        step, rep = general_body, "rep"
    in_specs = (
        P(rep, "exp", None),
        P(rep, "exp", None),
        P(rep, "exp", None),
        P(rep, "exp", None, None),
        P("exp", rep, None),
        P("exp", rep, None),
        P("exp", rep, None),
    )
    out_specs = (
        P(rep, "exp", None),
        P(rep, "exp", None),
        P("exp", rep, None),
        P("exp", rep, None),
        P("exp", rep, None),
    )
    return jax.shard_map(step, mesh=mesh, in_specs=in_specs, out_specs=out_specs, check_vma=False)
```

```python
import jax
import jax.numpy as jnp
from jax import lax
from jax.experimental import pallas as pl
from jax.experimental.pallas import tpu as pltpu
from jax.sharding import Mesh
from jax.sharding import PartitionSpec as P

TOPK = 8
EXP_DEV = 4
PARTS = 4
CUT = 3
CAP = 8
LANES = 128
F32 = jnp.float32
BF16 = jnp.bfloat16


def dot(left, right, ldim, rdim):
    return lax.dot_general(
        left, right, (((ldim,), (rdim,)), ((), ())), preferred_element_type=F32
    )


def call(kernel, *args, out, scratch=(), space=pltpu.VMEM, busy_us=None):
    spec = pl.BlockSpec(memory_space=pltpu.VMEM)
    return pl.pallas_call(
        kernel,
        out_shape=[jax.ShapeDtypeStruct(s, d) for s, d in out],
        in_specs=[pl.BlockSpec(memory_space=space)] * len(args),
        out_specs=[spec] * len(out),
        scratch_shapes=list(scratch),
        cost_estimate=busy_us and pl.CostEstimate(
            flops=busy_us * 10**9, transcendentals=0, bytes_accessed=busy_us * 3 * 10**6
        ),
        compiler_params=pltpu.CompilerParams(vmem_limit_bytes=32 << 20),
    )(*args)


def in_hbm(*arrays):
    return [pltpu.with_memory_space_constraint(a, pltpu.HBM) for a in arrays]


def fetch(sources, targets, sems):
    copies = [
        pltpu.make_async_copy(source, target, sems.at[n])
        for n, (source, target) in enumerate(zip(sources, targets))
    ]
    for copy in copies:
        copy.start()
    return copies


def position():
    return lax.axis_index("q"), lax.axis_index("p")


def block(index, size):
    return pl.ds(pl.multiple_of(index * size, size), size)


def spread_kernel(*refs):
    (gate_ref, up_ref, down_ref, saved_ref, ids_ref, scales_ref, grads_ref), refs = refs[:7], refs[7:]
    whole_ref, both_ref, last_ref, mine_ref, across_ref, *kept, saved, sems = refs
    hidden = gate_ref.shape[1]
    half = mine_ref.shape[1]
    q, _ = position()
    sources = (gate_ref, up_ref, down_ref)
    targets = (both_ref.at[:, :hidden], both_ref.at[:, hidden:], last_ref)
    again = [whole_ref.at[:, i * hidden : (i + 1) * hidden] for i in range(3)]
    copies = fetch(
        (saved_ref, *sources, *sources, ids_ref, scales_ref, grads_ref),
        (saved, *targets, *again, *kept),
        sems,
    )
    copies[0].wait()
    mine_ref[...] = saved[:, block(q, half)]
    across_ref[...] = saved[:, block(1 - q, half)]
    for copy in copies[1:]:
        copy.wait()


def route_kernel(ids_ref, scales_ref, grads_ref, send_ref, hits_ref):
    slots, tokens = hits_ref.shape
    owners = slots // CAP
    half = send_ref.shape[1]
    earlier = lax.broadcasted_iota(jnp.int32, (tokens, tokens), 0) < (
        lax.broadcasted_iota(jnp.int32, (tokens, tokens), 1)
    )
    before = jnp.where(earlier, 1.0, 0.0).astype(BF16)
    slot = lax.broadcasted_iota(jnp.int32, (CAP, tokens), 0).astype(F32)
    ids = ids_ref[...]
    weights = scales_ref[...].astype(F32)
    hits, scales = [], []
    for j in range(owners):
        match = ids == j * EXP_DEV
        hits.append(jnp.sum(jnp.where(match, 1.0, 0.0), axis=0, keepdims=True))
        scales.append(jnp.sum(jnp.where(match, weights, 0.0), axis=0, keepdims=True))
    pad = [jnp.zeros((1, tokens), F32)] * (-owners % 8)
    hit = jnp.concatenate(hits + pad, axis=0)
    place = dot(hit.astype(BF16), before, 1, 0)
    chosen, scaled = [], []
    for j in range(owners):
        here = (place[j : j + 1] == slot) & (hits[j] > 0.0)
        chosen.append(jnp.where(here, 1.0, 0.0))
        scaled.append(jnp.where(here, scales[j], 0.0))
    hits_ref[...] = jnp.concatenate(chosen, axis=0)
    picks = jnp.concatenate(scaled, axis=0).astype(BF16)
    rows = dot(picks, grads_ref[...], 1, 0).astype(BF16)
    for h in range(2):
        send_ref[h * slots : (h + 1) * slots, :] = rows[:, h * half : (h + 1) * half]


def gate_up_kernel(mine_ref, theirs_ref, *refs):
    weights, (pair_ref, own_ref, sent_ref) = refs[:PARTS], refs[PARTS:]
    q, p = position()
    slots = mine_ref.shape[0]
    width = weights[0].shape[0]
    pair_ref[block(q, slots), :] = mine_ref[...]
    pair_ref[block(1 - q, slots), :] = theirs_ref[...]
    total = None
    for k in range(PARTS):
        columns = weights[k][:, : own_ref.shape[1]]
        term = dot(pair_ref[:, block(p ^ k, width)], columns, 1, 0)
        total = term if total is None else total + term
    own_ref[...] = total
    sent_ref[...] = total.astype(BF16)


def down_kernel(routed_ref, *refs):
    weights, (own_ref, sent_ref) = refs[:PARTS], refs[PARTS:]
    _, p = position()
    width = weights[0].shape[0]
    total = None
    for k in range(PARTS):
        columns = weights[k][:, weights[k].shape[1] - own_ref.shape[1] :]
        term = dot(routed_ref[:, block(p ^ k, width)], columns, 1, 0)
        total = term if total is None else total + term
    own_ref[...] = total
    sent_ref[...] = total.astype(BF16)


def delta_kernel(gate_up_ref, other_ref, down_ref, down_other_ref, pair_ref, routed_ref, *refs):
    weights, kept_ref, swap_ref, sends = refs[:PARTS], refs[PARTS], refs[PARTS + 1], refs[PARTS + 2 : -1]
    back_ref = refs[-1]
    q, p = position()
    width = weights[0].shape[0]
    hidden_width = down_ref.shape[1]
    half = pair_ref.shape[1]
    both = gate_up_ref[...] + other_ref[...].astype(F32)
    hidden_grad = down_ref[...] + down_other_ref[...].astype(F32)
    pre_gate, pre_up = both[:, :hidden_width], both[:, hidden_width:]
    sigmoid = jax.nn.sigmoid(pre_gate)
    activated = pre_gate * sigmoid
    hidden = (activated * pre_up).astype(BF16)
    gate_delta = hidden_grad * pre_up * sigmoid * (1.0 + pre_gate * (1.0 - sigmoid))
    gate_delta = gate_delta.astype(BF16)
    up_delta = (hidden_grad * activated).astype(BF16)
    route = jnp.sum(hidden.astype(F32) * hidden_grad, axis=1, keepdims=True)
    back_ref[:, half:] = jnp.broadcast_to(route, (route.shape[0], LANES)).astype(BF16)
    for k in range(PARTS):
        lanes = block(p ^ k, width)
        back_ref[:, lanes] = (
            dot(gate_delta, weights[k][:, :hidden_width], 1, 1)
            + dot(up_delta, weights[k][:, hidden_width : 2 * hidden_width], 1, 1)
        ).astype(BF16)
        sends[k][:, :hidden_width] = gate_delta
        sends[k][:, hidden_width : 2 * hidden_width] = up_delta
        sends[k][:, 2 * hidden_width : 3 * hidden_width] = hidden
        sends[k][:, 3 * hidden_width : 3 * hidden_width + width] = pair_ref[:, lanes]
        sends[k][:, 3 * hidden_width + width :] = routed_ref[:, lanes]
    slots = kept_ref.shape[0]
    kept_ref[...] = back_ref[block(q, slots), :]
    swap_ref[...] = back_ref[block(1 - q, slots), :]


def return_kernel(kept_ref, swap_ref, *refs):
    outs, rows_ref = refs[:-1], refs[-1]
    q, _ = position()
    half = kept_ref.shape[1] - LANES
    rows_ref[:, block(q, half)] = kept_ref[:, :half].astype(F32)
    rows_ref[:, block(1 - q, half)] = swap_ref[:, :half].astype(F32)
    rows_ref[:, 2 * half :] = kept_ref[:, half:].astype(F32)
    for m, out in enumerate(outs):
        out[...] = rows_ref[block(lax.axis_index("exp") ^ m, CAP), :].astype(BF16)


def grads_step(replicas):
    def grads_kernel(*refs):
        parts, (gate_ref, up_ref, down_ref) = refs[:PARTS], refs[PARTS:]
        width, hidden = gate_ref.shape

        def column(start, size):
            return jnp.concatenate([part[:, start : start + size] for part in parts], axis=0)

        both = dot(column(3 * hidden, width), column(0, 2 * hidden), 0, 0) / replicas
        gate_ref[...] = both[:, :hidden]
        up_ref[...] = both[:, hidden:]
        down = dot(column(3 * hidden + width, width), column(2 * hidden, hidden), 0, 0)
        down_ref[...] = down / replicas

    return grads_kernel


def tokens_kernel(ids_ref, scales_ref, hits_ref, *refs):
    pieces, (input_grad_ref, route_ref) = refs[:-2], refs[-2:]
    features = input_grad_ref.shape[1]
    ids = ids_ref[...]
    out = jnp.zeros(ids.shape, F32)
    hits = []
    for m, piece in enumerate(pieces):
        expert = lax.axis_index("exp") ^ m
        hits.append(hits_ref[block(expert, CAP), :])
        value = jnp.sum(hits[m] * piece[:, features:].astype(F32), axis=0, keepdims=True)
        out = jnp.where(ids == expert * EXP_DEV, value, out)
    route_ref[...] = (out / scales_ref[...].astype(F32)).astype(BF16)
    rows = jnp.concatenate([piece[:, :features].astype(F32) for piece in pieces], axis=0)
    hits = jnp.concatenate(hits, axis=0)
    input_grad_ref[...] = dot(hits.astype(BF16), rows.astype(BF16), 0, 0).astype(BF16)


def body(expert_ids, route_weights, out_grad, saved_inputs, gate_weight, up_weight, down_weight):
    owners = lax.axis_size("exp")
    replicas = lax.axis_size("q") * PARTS
    tokens, features = out_grad.shape[1:]
    slots = saved_inputs.shape[2]
    width, hidden_width = gate_weight.shape[1:]
    half, rows = features // 2, 2 * slots

    def in_half(value, mask):
        return lax.ppermute(value, "p", [(i, i ^ mask) for i in range(PARTS)])

    def across_halves(value):
        return lax.ppermute(value, "q", [(0, 1), (1, 0)])

    def exchange(value):
        blocks = value.reshape(2 * owners, CAP, value.shape[1])
        return lax.all_to_all(blocks, ("q", "exp"), 0, 0, tiled=True).reshape(value.shape)

    whole, both, last, mine, across, ids, scales, grads = call(
        spread_kernel,
        *in_hbm(gate_weight[0], up_weight[0], down_weight[0], saved_inputs[0, 0]),
        *in_hbm(expert_ids[0].T, route_weights[0].T, out_grad[0]),
        out=[((width, n * hidden_width), BF16) for n in (3, 2, 1)]
        + [((slots, half), BF16)] * 2
        + [((TOPK, tokens), jnp.int32), ((TOPK, tokens), BF16), ((tokens, features), BF16)],
        scratch=[pltpu.VMEM((slots, features), BF16), pltpu.SemaphoreType.DMA((10,))],
        space=pltpu.HBM,
    )
    theirs = across_halves(across)
    wholes = {k: in_half(whole, k) for k in range(1, PARTS) if k != CUT}
    both = [both] + [wholes[k] if k in wholes else in_half(both, k) for k in range(1, PARTS)]
    last = [last] + [wholes[k] if k in wholes else in_half(last, k) for k in range(1, PARTS)]
    sent, hits = call(
        route_kernel,
        ids,
        scales,
        grads,
        out=[((rows, half), BF16), ((slots, tokens), F32)],
    )
    routed = exchange(sent)
    pair, gate_up, partial = call(
        gate_up_kernel,
        mine,
        theirs,
        *both,
        busy_us=5,
        out=[
            ((rows, half), BF16),
            ((rows, 2 * hidden_width), F32),
            ((rows, 2 * hidden_width), BF16),
        ],
    )
    other = across_halves(partial)
    down, partial = call(
        down_kernel,
        routed,
        *last,
        out=[((rows, hidden_width), F32), ((rows, hidden_width), BF16)],
    )
    kept, swapped, *sends = call(
        delta_kernel,
        gate_up,
        other,
        down,
        across_halves(partial),
        pair,
        routed,
        *both,
        out=[((slots, half + LANES), BF16)] * 2
        + [((rows, 3 * hidden_width + 2 * width), BF16)] * PARTS,
        scratch=[pltpu.VMEM((rows, half + LANES), BF16)],
    )
    pieces = call(
        return_kernel,
        kept,
        across_halves(swapped),
        busy_us=3,
        out=[((CAP, features + LANES), BF16)] * owners,
        scratch=[pltpu.VMEM((slots, features + LANES), F32)],
    )
    pieces = [pieces[0]] + [
        lax.ppermute(pieces[m], "exp", [(i, i ^ m) for i in range(owners)])
        for m in range(1, owners)
    ]
    sends = [sends[0]] + [in_half(sends[k], k) for k in (3, 2, 1)]
    gate_grad, up_grad, down_grad = call(
        grads_step(replicas), *sends, out=[((width, hidden_width), F32)] * 3
    )
    input_grad, route_grad = call(
        tokens_kernel,
        ids,
        scales,
        hits,
        *pieces,
        out=[((tokens, features), BF16), ((TOPK, tokens), BF16)],
    )
    return (input_grad[None], route_grad.T[None], gate_grad[None], up_grad[None], down_grad[None])


def slot_table(block_ids, slot_count, owners):
    flat_ids = block_ids.reshape(-1)
    chosen = flat_ids % EXP_DEV == 0
    owner_of = flat_ids // EXP_DEV
    capacity = slot_count // owners
    onehot = ((owner_of[:, None] == jnp.arange(owners)[None, :]) & chosen[:, None]).astype(
        jnp.int32
    )
    earlier = jnp.cumsum(onehot, axis=0) - onehot
    position = jnp.sum(earlier * onehot, axis=1)
    slot_of = jnp.where(chosen, owner_of * capacity + position, -1)
    return slot_of[None, :] == jnp.arange(slot_count)[:, None]


def first_contract(left, right):
    return lax.dot_general(
        left, right, (((0,), (0,)), ((), ())), preferred_element_type=jnp.float32
    )


def second_contract(left, right):
    return lax.dot_general(
        left, right, (((1,), (1,)), ((), ())), preferred_element_type=jnp.float32
    )


def general_body(expert_ids, route_weights, out_grad, saved_inputs, gate_weight, up_weight, down_weight):
    owners = lax.axis_size("exp")
    replicas = lax.axis_size("rep")
    tokens_here = out_grad.shape[1]
    features = out_grad.shape[2]
    hidden_width = gate_weight.shape[2]
    slot_count = saved_inputs.shape[2]
    capacity = slot_count // owners
    placed = slot_table(expert_ids[0], slot_count, owners)
    weights_flat = route_weights[0].reshape(-1)
    slot_scale = jnp.sum(
        jnp.where(placed, weights_flat[None, :], jnp.zeros((), weights_flat.dtype)), axis=1
    )
    token_hits = jnp.any(placed.reshape(slot_count, tokens_here, TOPK), axis=2)
    token_of = jnp.sum(jnp.where(token_hits, jnp.arange(tokens_here)[None, :], 0), axis=1)
    is_live = jnp.any(token_hits, axis=1)
    routed = jnp.where(is_live[:, None], out_grad[0][token_of], jnp.zeros((), jnp.bfloat16))
    arrived, arrived_scale = (
        lax.all_to_all(
            routed.reshape(owners, capacity, features),
            "exp",
            split_axis=0,
            concat_axis=0,
            tiled=True,
        ),
        lax.all_to_all(
            slot_scale.reshape(owners, capacity), "exp", split_axis=0, concat_axis=0, tiled=True
        ),
    )
    full_gate, full_up, full_down = (
        lax.all_gather(gate_weight[0], "rep", axis=0, tiled=True),
        lax.all_gather(up_weight[0], "rep", axis=0, tiled=True),
        lax.all_gather(down_weight[0], "rep", axis=0, tiled=True),
    )
    grad_rows = arrived.reshape(slot_count, features)
    scale_col = arrived_scale.reshape(slot_count, 1).astype(jnp.float32)
    inputs_here = saved_inputs[0, 0]
    pre_gate = jnp.dot(inputs_here, full_gate, preferred_element_type=jnp.float32)
    pre_up = jnp.dot(inputs_here, full_up, preferred_element_type=jnp.float32)
    sigmoid_gate = jax.nn.sigmoid(pre_gate)
    activated = pre_gate * sigmoid_gate
    hidden = (activated * pre_up).astype(jnp.bfloat16)
    raw_grad = jnp.dot(grad_rows, full_down, preferred_element_type=jnp.float32)
    slot_route = jnp.sum(hidden.astype(jnp.float32) * raw_grad, axis=1).astype(jnp.bfloat16)
    hidden_grad = scale_col * raw_grad
    scaled_rows = (scale_col * grad_rows.astype(jnp.float32)).astype(jnp.bfloat16)
    gate_delta = (
        hidden_grad * pre_up * sigmoid_gate * (1.0 + pre_gate * (1.0 - sigmoid_gate))
    ).astype(jnp.bfloat16)
    up_delta = (hidden_grad * activated).astype(jnp.bfloat16)
    back_rows = (
        second_contract(gate_delta, full_gate) + second_contract(up_delta, full_up)
    ).astype(jnp.bfloat16)
    returned, returned_route = (
        lax.all_to_all(
            back_rows.reshape(owners, capacity, features),
            "exp",
            split_axis=0,
            concat_axis=0,
            tiled=True,
        ),
        lax.all_to_all(
            slot_route.reshape(owners, capacity), "exp", split_axis=0, concat_axis=0, tiled=True
        ),
    )
    returned_flat = returned.reshape(slot_count, features)
    route_flat = returned_route.reshape(slot_count)
    combined = jax.ops.segment_sum(
        jnp.where(is_live[:, None], returned_flat.astype(jnp.float32), 0.0),
        token_of,
        num_segments=tokens_here,
    )
    input_grad = combined.astype(jnp.bfloat16)[None]
    route_grad = jnp.sum(
        jnp.where(placed, route_flat[:, None], jnp.zeros((), jnp.bfloat16)), axis=0
    )
    route_grad = route_grad.reshape(1, tokens_here, TOPK)
    joined_share = lax.psum_scatter(
        jnp.concatenate(
            [
                jnp.concatenate(
                    [
                        first_contract(inputs_here, gate_delta),
                        first_contract(inputs_here, up_delta),
                    ],
                    axis=1,
                ),
                first_contract(scaled_rows, hidden),
            ],
            axis=1,
        ),
        "rep",
        scatter_dimension=0,
        tiled=True,
    )
    gate_share = joined_share[:, :hidden_width]
    up_share = joined_share[:, hidden_width : 2 * hidden_width]
    down_share = joined_share[:, 2 * hidden_width :]
    gate_grad = (gate_share / replicas)[None]
    up_grad = (up_share / replicas)[None]
    down_grad = (down_share / replicas)[None]
    return (input_grad, route_grad, gate_grad, up_grad, down_grad)


def solution(mesh):
    replicas, owners = mesh.shape["rep"], mesh.shape["exp"]
    if replicas == 2 * PARTS:
        step, rep = body, ("q", "p")
        mesh = Mesh(mesh.devices.reshape(2, PARTS, owners), ("q", "p", "exp"))
    else:
        step, rep = general_body, "rep"
    in_specs = (
        P(rep, "exp", None),
        P(rep, "exp", None),
        P(rep, "exp", None),
        P(rep, "exp", None, None),
        P("exp", rep, None),
        P("exp", rep, None),
        P("exp", rep, None),
    )
    out_specs = (
        P(rep, "exp", None),
        P(rep, "exp", None),
        P("exp", rep, None),
        P("exp", rep, None),
        P("exp", rep, None),
    )
    return jax.shard_map(step, mesh=mesh, in_specs=in_specs, out_specs=out_specs, check_vma=False)
```
